512 devices in a mesh: space: 32 (over z_hi, x, core), chan: 16 (over z_lo, y).
Axes of the slice: x: 4, y: 8, z: 8 (z_hi: 4, z_lo: 2; z = z_hi * 2 + z_lo), core: 2. Of those that a mesh axis runs over, the one named last changes fastest.
Arguments:
- volume: bfloat16 [128, 128, 16, 128], P('chan', 'space'), may hold values from -6 to 6
- kernel: bfloat16 [128, 3, 3, 3, 128], P('chan'), may hold values from -0.109375 to 0.109375
- upstream: bfloat16 [128, 32, 4, 32], P('chan', 'space'), may hold values from -24 to 24
Outputs:
- pooled: bfloat16 [128, 32, 4, 32], P('chan', 'space')
- volume_grad: bfloat16 [128, 128, 16, 128], P('chan', 'space')
- kernel_grad: float32 [128, 3, 3, 3, 128], P('chan')
The draws below stay inside these ranges and needn't reach their ends.
All inputs are finite; a program needn't handle non-finite values.
Results may differ from the reference program's by a relative error of at most 0.013.
Values may be sent and summed in bfloat16 or wider, within the bound.
A program may use at most 64 MiB of HBM per device.

```python
import jax
import jax.numpy as jnp
from jax import lax

CIN = 128
COUT = 128
HGT = 16
WID = 128
DEPTH = 128


def block_levels(stream_key, shape, cuts, smallest, top_value):
    level, own = 1.0, jax.random.fold_in(stream_key, 6)
    for dim, blocks in cuts:
        heights = jnp.exp(jax.random.uniform(jax.random.fold_in(own, dim), (blocks,), jnp.float32, smallest / len(cuts), top_value / len(cuts)))
        level = level * jnp.repeat(heights, shape[dim] // blocks).reshape([-1 if axis == dim else 1 for axis in range(len(shape))])
    return level


def scatter_about(rng, extent, scale, limit, pieces=(), dtype=jnp.bfloat16):
    result = jax.random.normal(rng, extent, jnp.float32) * scale
    if len(pieces) > 0:
        result = block_levels(rng, extent, pieces, -0.22, 0.18) * result
    return jnp.clip(result, min=-limit, max=limit).astype(dtype)


def setup_inputs(seed: int = 0) -> dict:
    key_of = jax.random.split(jax.random.key(seed), 4)
    return {
        "volume": scatter_about(key_of[0], (CIN, DEPTH, HGT, WID), 1.0, 6.0, ((0, 16), (1, 32))),
        "kernel": scatter_about(key_of[1], (CIN, 3, 3, 3, COUT), (CIN * 27) ** -0.5, 0.109375, ((0, 16),)),
        "upstream": scatter_about(key_of[2], (COUT, DEPTH // 4, HGT // 4, WID // 4), 4.0, 24.0, ((0, 16), (1, 32))),
    }


slope_neg = 0.3


def reference(volume, kernel, upstream):
    vol_f = volume.astype(jnp.float32)
    ker_f = kernel.astype(jnp.float32)
    pre = lax.conv_general_dilated(vol_f[None], ker_f, (2, 2, 2), ((1, 1), (1, 1), (1, 1)), dimension_numbers=("NCDHW", "IDHWO", "NCDHW"), precision=lax.Precision.HIGHEST)[0]
    activated = jnp.where(pre > 0, pre, slope_neg * pre)
    chans, depth_out, rows_out, cols_out = pre.shape
    blocks = activated.reshape(chans, depth_out // 2, 2, rows_out // 2, 2, cols_out // 2, 2)
    pooled = jnp.mean(blocks, axis=(2, 4, 6)).astype(jnp.bfloat16)
    spread = upstream.astype(jnp.float32) * 0.125
    spread = jnp.broadcast_to(spread[:, :, None, :, None, :, None], blocks.shape).reshape(pre.shape)
    pre_grad = (spread * jnp.where(pre > 0, 1.0, slope_neg)).astype(jnp.bfloat16)
    grad_f = pre_grad.astype(jnp.float32)
    flipped = ker_f[:, ::-1, ::-1, ::-1, :]
    volume_grad = lax.conv_general_dilated(grad_f[None], flipped, (1, 1, 1), ((1, 2), (1, 2), (1, 2)), lhs_dilation=(2, 2, 2), dimension_numbers=("NCDHW", "ODHWI", "NCDHW"), precision=lax.Precision.HIGHEST)[0].astype(jnp.bfloat16)
    kernel_grad = lax.conv_general_dilated(vol_f[None], grad_f[None], (1, 1, 1), ((1, 0), (1, 0), (1, 0)), rhs_dilation=(2, 2, 2), dimension_numbers=("CNDHW", "IODHW", "NDHWC"), precision=lax.Precision.HIGHEST)
    return pooled, volume_grad, kernel_grad
```

```python
import jax
import jax.numpy as jnp
from jax import lax
from jax.experimental import pallas as pl
from jax.experimental.pallas import tpu as pltpu
from jax.sharding import PartitionSpec as P

slope_neg = 0.3
MESH = pl.DeviceIdType.MESH
bf16, f32, i32 = jnp.bfloat16, jnp.float32, jnp.int32


def iota(shape, dim):
    return lax.broadcasted_iota(i32, shape, dim)


def one_hot(condition):
    return jnp.where(condition, 1.0, 0.0).astype(bf16)


def row_picker():
    out, inn = iota((160, 128), 0), iota((160, 128), 1)
    same = (out & 7) == (inn >> 4)
    return one_hot(same & ((inn & 15) == 4 * ((out >> 3) & 3) + (out >> 5) - 1))


def column_picker():
    inn, out = iota((256, 384), 0), iota((256, 384), 1)
    same = (inn >> 7) == ((out >> 6) & 1)
    return one_hot(same & ((inn & 127) == 2 * (out & 63) + (out >> 7) - 1))


def pool_picker():
    coarse, fine = iota((128, 1024), 0), iota((128, 1024), 1)
    return one_hot(
        ((coarse >> 5) == ((fine >> 7) & 3)) & ((coarse & 31) == ((fine >> 1) & 31))
    )


def channel_first():
    out, inn = iota((128, 128), 0), iota((128, 128), 1)
    return one_hot(((out >> 4) == (inn & 7)) & ((out & 15) == (inn >> 3)))


def front_kernel(vol, rim, weights, up, part, taps, spread, stage):
    pick_rows = row_picker()
    pick_cols = column_picker()
    planes = []
    for p in range(5):
        plane = rim[:, 0] if p == 0 else vol[:, p - 1]
        rows = jnp.dot(pick_rows, plane.reshape(128, 128), preferred_element_type=f32)
        planes.append(rows.astype(bf16))
    for b in range(3):
        pairs = jnp.concatenate(
            [
                jnp.concatenate(
                    [u[32 * b : 32 * b + 32], u[32 * b + 64 : 32 * b + 96]], axis=1
                )
                for u in planes
            ],
            axis=0,
        )
        picked = jnp.dot(pairs, pick_cols, preferred_element_type=f32)
        for e in range(3):
            for a in range(3):
                for z in range(2):
                    for yh in range(4):
                        src = ((2 * z + a) * 4 + yh) * 8
                        dst = ((b * 3 + e) * 3 + a) * 8
                        lane = (z * 4 + yh) * 128
                        stage[dst : dst + 8, lane : lane + 128] = picked[
                            src : src + 8, e * 128 : e * 128 + 128
                        ]
    columns = stage[...].astype(bf16)
    taps[...] = columns
    part[...] = lax.dot_general(
        weights[...], columns, (((0,), (0,)), ((), ())), preferred_element_type=f32
    ).reshape(16, 8, 1024)
    spread[...] = jnp.dot(up[...], pool_picker(), preferred_element_type=f32) * 0.125


def everyone(axis, n):
    me = lax.axis_index(axis)
    barrier = pltpu.get_barrier_semaphore()
    for k in range(1, n):
        pl.semaphore_signal(
            barrier, inc=1, device_id={axis: lax.rem(me + k, n)}, device_id_type=MESH
        )
    pl.semaphore_wait(barrier, n - 1)
    return me


def chan_kernel(n, part, spread, pre_out, panel_out, got, panel, s1, r1, s2, r2):
    me = everyone("chan", n)
    copies = []
    for k in range(1, n):
        peer = lax.rem(me + k, n)
        copy = pltpu.make_async_remote_copy(
            src_ref=part.at[peer],
            dst_ref=got.at[k],
            send_sem=s1.at[k],
            recv_sem=r1.at[k],
            device_id={"chan": peer},
            device_id_type=MESH,
        )
        copy.start()
        copies.append(copy)
    pre = part[me]
    for k in range(1, n):
        copies[k - 1].wait_recv()
        pre = pre + got[k]
    pre_out[...] = pre
    grad = (spread[...] * jnp.where(pre > 0, 1.0, slope_neg)).astype(bf16)
    panel[me] = grad
    gathers = []
    for k in range(1, n):
        copy = pltpu.make_async_remote_copy(
            src_ref=panel.at[me],
            dst_ref=panel.at[me],
            send_sem=s2.at[k],
            recv_sem=r2.at[k],
            device_id={"chan": lax.rem(me + k, n)},
            device_id_type=MESH,
        )
        copy.start()
        gathers.append(copy)
    for copy in copies:
        copy.wait_send()
    for copy in gathers:
        copy.wait_recv()
    panel_out[...] = panel[...]
    for copy in gathers:
        copy.wait_send()


def weight_kernel(taps, panel, out):
    grads = panel[...].reshape(128, 1024)
    total = lax.dot_general(
        taps[...], grads, (((1,), (1,)), ((), ())), preferred_element_type=f32
    )
    out[0:27] = total.reshape(27, 8, 128)
    out[27:32] = jnp.zeros((5, 8, 128), f32)


def volume_kernel(weights, panel, rim, pre, out, pooled, terms, rows, fold):
    pick_cols = column_picker()
    w = weights[...]
    terms[:, 0:1024] = jnp.dot(w, panel[...].reshape(128, 1024), preferred_element_type=f32)
    terms[:, 1024:1536] = jnp.dot(w, rim[...].reshape(128, 512), preferred_element_type=f32)
    for b in range(3):
        for a in range(3):
            for zi in range(2):
                z = zi + 1 if a == 0 else zi
                for yh in range(4):
                    dst = (((b * 3 + a) * 2 + zi) * 4 + yh) * 8
                    lane = (z * 4 + yh) * 128
                    for e in range(3):
                        src = ((b * 3 + e) * 3 + a) * 8
                        rows[dst : dst + 8, e * 128 : e * 128 + 128] = terms[
                            src : src + 8, lane : lane + 128
                        ]
    high = rows[...].astype(bf16)
    low = (rows[...] - high.astype(f32)).astype(bf16)
    dims = (((1,), (1,)), ((), ()))
    fold[...] = lax.dot_general(high, pick_cols, dims, preferred_element_type=f32)
    fold[...] += lax.dot_general(low, pick_cols, dims, preferred_element_type=f32)
    order = channel_first()
    depth_terms = (((1, 0),), ((2, 0), (0, 0)), ((1, 1),), ((2, 1), (0, 1)))
    for i in range(4):
        sums = []
        for j in range(16):
            if j % 2 == 0:
                row_terms = ((1, j // 2),)
            elif j < 15:
                row_terms = ((2, j // 2), (0, j // 2 + 1))
            else:
                row_terms = ((2, j // 2),)
            acc = None
            for a, zi in depth_terms[i]:
                for b, y in row_terms:
                    src = (((b * 3 + a) * 2 + zi) * 4 + y // 2) * 8
                    lane = (y % 2) * 128
                    term = fold[src : src + 8, lane : lane + 128]
                    acc = term if acc is None else acc + term
            sums.append(acc)
        plane = jnp.concatenate(sums, axis=0).astype(bf16)
        moved = jnp.dot(order, plane, preferred_element_type=f32).astype(bf16)
        out[:, i] = moved.reshape(8, 16, 128)
    act = jnp.where(pre[...] > 0, pre[...], slope_neg * pre[...])
    first = act.astype(bf16)
    rest = act - first.astype(f32)
    second = rest.astype(bf16)
    third = (rest - second.astype(f32)).astype(bf16)
    pick = pool_picker()
    total = sum(
        lax.dot_general(piece, pick, dims, preferred_element_type=f32)
        for piece in (third, second, first)
    )
    pooled[...] = (total * 0.125).astype(bf16)


def space_kernel(n, terms, out, got, mine, s1, r1, s2, r2):
    me = everyone("space", n)
    copies = []
    for k in range(1, n):
        peer = lax.rem(me + k, n)
        copy = pltpu.make_async_remote_copy(
            src_ref=terms.at[peer],
            dst_ref=got.at[k],
            send_sem=s1.at[k],
            recv_sem=r1.at[k],
            device_id={"space": peer},
            device_id_type=MESH,
        )
        copy.start()
        copies.append(copy)
    total = terms[me]
    for k in range(1, n):
        copies[k - 1].wait_recv()
        total = total + got[k]
    mine[me] = total
    gathers = []
    for k in range(1, n):
        copy = pltpu.make_async_remote_copy(
            src_ref=mine.at[me],
            dst_ref=mine.at[me],
            send_sem=s2.at[k],
            recv_sem=r2.at[k],
            device_id={"space": lax.rem(me + k, n)},
            device_id_type=MESH,
        )
        copy.start()
        gathers.append(copy)
    for copy in copies:
        copy.wait_send()
    for copy in gathers:
        copy.wait_recv()
    out[...] = mine[...]
    for copy in gathers:
        copy.wait_send()


def in_vmem(count):
    return [pl.BlockSpec(memory_space=pltpu.VMEM)] * count


def shaped(*shape, dtype=f32):
    return jax.ShapeDtypeStruct(shape, dtype)


def front(vol, rim, weights, up):
    return pl.pallas_call(
        front_kernel,
        out_shape=(
            shaped(16, 8, 1024),
            shaped(216, 1024, dtype=bf16),
            shaped(8, 1024),
        ),
        in_specs=in_vmem(4),
        out_specs=tuple(in_vmem(3)),
        scratch_shapes=[pltpu.VMEM((216, 1024), f32)],
        cost_estimate=pl.CostEstimate(flops=200_000_000, bytes_accessed=1_500_000, transcendentals=0),
    )(vol, rim, weights, up)


def chan_exchange(part, spread):
    n = lax.axis_size("chan")
    sem = pltpu.SemaphoreType.DMA((n,))
    return pl.pallas_call(
        lambda *refs: chan_kernel(n, *refs),
        name="chan_exchange",
        out_shape=(shaped(8, 1024), shaped(n, 8, 1024, dtype=bf16)),
        in_specs=in_vmem(2),
        out_specs=tuple(in_vmem(2)),
        scratch_shapes=[
            pltpu.VMEM((n, 8, 1024), f32),
            pltpu.VMEM((n, 8, 1024), bf16),
            sem,
            sem,
            sem,
            sem,
        ],
        compiler_params=pltpu.CompilerParams(collective_id=0, has_side_effects=True),
    )(part, spread)


def weight_grad(taps, panel):
    return pl.pallas_call(
        weight_kernel,
        out_shape=shaped(32, 8, 128),
        in_specs=in_vmem(2),
        out_specs=in_vmem(1)[0],
        cost_estimate=pl.CostEstimate(flops=200_000_000, bytes_accessed=1_500_000, transcendentals=0),
    )(taps, panel)


def volume_grad(weights, panel, rim, pre):
    return pl.pallas_call(
        volume_kernel,
        out_shape=(shaped(8, 4, 16, 128, dtype=bf16), shaped(8, 128, dtype=bf16)),
        in_specs=in_vmem(4),
        out_specs=tuple(in_vmem(2)),
        scratch_shapes=[
            pltpu.VMEM((216, 1536), f32),
            pltpu.VMEM((576, 384), f32),
            pltpu.VMEM((576, 256), f32),
        ],
        cost_estimate=pl.CostEstimate(flops=400_000_000, bytes_accessed=3_000_000, transcendentals=0),
    )(weights, panel, rim, pre)


def space_sum(terms):
    n = lax.axis_size("space")
    sem = pltpu.SemaphoreType.DMA((n,))
    return pl.pallas_call(
        lambda *refs: space_kernel(n, *refs),
        name="space_sum",
        out_shape=shaped(n, 8, 128),
        in_specs=in_vmem(1),
        out_specs=in_vmem(1)[0],
        scratch_shapes=[
            pltpu.VMEM((n, 8, 128), f32),
            pltpu.VMEM((n, 8, 128), f32),
            sem,
            sem,
            sem,
            sem,
        ],
        compiler_params=pltpu.CompilerParams(collective_id=1, has_side_effects=True),
    )(terms)


def from_behind(block, axis, distance):
    devices = range(lax.axis_size(axis))
    route = [(i - distance, i) for i in devices if i - distance in devices]
    return lax.ppermute(block, axis, route)


def on_device(volume, kernel, upstream):
    lower_rim = from_behind(volume[:, -1:], "space", 1)
    weights = kernel.transpose(2, 3, 1, 0, 4).reshape(216, 128)
    part, taps, spread = front(volume, lower_rim, weights, upstream.reshape(8, 128))
    pre, panel = chan_exchange(part, spread)
    upper_rim = from_behind(panel[:, :, :512], "space", -1)
    terms = weight_grad(taps, panel)
    input_grad, pooled = volume_grad(weights, panel, upper_rim, pre)
    total = space_sum(terms)
    kernel_grad = total[:27].reshape(3, 3, 3, 8, 128).transpose(3, 2, 0, 1, 4)
    return pooled.reshape(upstream.shape), input_grad, kernel_grad


def solution(mesh):
    return jax.shard_map(
        on_device,
        mesh=mesh,
        in_specs=(
            P("chan", "space", None, None),
            P("chan", None, None, None, None),
            P("chan", "space", None, None),
        ),
        out_specs=(
            P("chan", "space", None, None),
            P("chan", "space", None, None),
            P("chan", None, None, None, None),
        ),
        check_vma=False,
    )
```

```python
import jax
import jax.numpy as jnp
from jax import lax
from jax.experimental import pallas as pl
from jax.experimental.pallas import tpu as pltpu
from jax.sharding import PartitionSpec as P

slope_neg = 0.3
MESH = pl.DeviceIdType.MESH
bf16, f32, i32 = jnp.bfloat16, jnp.float32, jnp.int32


def iota(shape, dim):
    return lax.broadcasted_iota(i32, shape, dim)


def one_hot(condition):
    return jnp.where(condition, 1.0, 0.0).astype(bf16)


def row_picker():
    out, inn = iota((160, 128), 0), iota((160, 128), 1)
    same = (out & 7) == (inn >> 4)
    return one_hot(same & ((inn & 15) == 4 * ((out >> 3) & 3) + (out >> 5) - 1))


def column_picker():
    inn, out = iota((256, 384), 0), iota((256, 384), 1)
    same = (inn >> 7) == ((out >> 6) & 1)
    return one_hot(same & ((inn & 127) == 2 * (out & 63) + (out >> 7) - 1))


def pool_picker():
    coarse, fine = iota((128, 1024), 0), iota((128, 1024), 1)
    return one_hot(
        ((coarse >> 5) == ((fine >> 7) & 3)) & ((coarse & 31) == ((fine >> 1) & 31))
    )


def channel_first():
    out, inn = iota((128, 128), 0), iota((128, 128), 1)
    row = 4 * ((inn >> 3) & 3) + (inn >> 5)
    return one_hot(((out >> 4) == (inn & 7)) & ((out & 15) == row))


def side_by_side(blocks):
    return jnp.concatenate(blocks, axis=1)


def block_kernel(
    n_space,
    vol,
    weights,
    up,
    pooled,
    grad_out,
    total_out,
    rim,
    stage,
    taps,
    part,
    from_z,
    z_sum,
    from_y,
    panel,
    rim_panel,
    folds,
    terms,
    got,
    mine,
    s_rim,
    r_rim,
    s_z,
    r_z,
    s_y,
    r_y,
    s_gy,
    r_gy,
    s_gz,
    r_gz,
    s_rs,
    r_rs,
    s_ag,
    r_ag,
):
    space, chan = lax.axis_index("space"), lax.axis_index("chan")
    half = lax.div(chan, 8)
    place = lax.rem(chan, 8)
    partner = lax.rem(chan + 8, 16)

    def along(k):
        return half * 8 + lax.rem(place + k, 8)

    def before(k):
        return half * 8 + lax.rem(place + 8 - k, 8)

    def ahead(k):
        return lax.rem(space + k, n_space)

    sent = []

    def send(src, dst, send_sem, recv_sem, **device):
        copy = pltpu.make_async_remote_copy(
            src_ref=src,
            dst_ref=dst,
            send_sem=send_sem,
            recv_sem=recv_sem,
            device_id=device,
            device_id_type=MESH,
        )
        copy.start()
        sent.append(copy)
        return copy

    barrier = pltpu.get_barrier_semaphore()
    for k in range(1, 8):
        pl.semaphore_signal(barrier, inc=1, device_id={"chan": along(k)}, device_id_type=MESH)
    pl.semaphore_signal(barrier, inc=1, device_id={"chan": partner}, device_id_type=MESH)
    for k in range(1, n_space):
        pl.semaphore_signal(barrier, inc=1, device_id={"space": ahead(k)}, device_id_type=MESH)

    pick_rows = row_picker()
    pick_cols = column_picker()

    def rows_of(plane):
        return jnp.dot(pick_rows, plane.reshape(128, 128), preferred_element_type=f32)

    planes = [None] + [rows_of(vol[:, p]).astype(bf16) for p in range(4)]
    pl.semaphore_wait(barrier, 8 + n_space - 1)
    rim_copy = send(vol.at[:, 3], rim, s_rim.at[0], r_rim.at[0], space=ahead(1))

    far_first = (4, 3, 5, 2, 6, 1, 7)
    w = weights[...]
    z_copies = {}
    for h in (1, 0):
        if h == 0:
            rim_copy.wait_recv()
            planes[0] = jnp.where(space > 0, rows_of(rim[...]), 0.0).astype(bf16)
        for b in range(3):
            pairs = jnp.concatenate(
                [
                    side_by_side([u[32 * b : 32 * b + 32], u[32 * b + 64 : 32 * b + 96]])
                    for u in planes[2 * h : 2 * h + 3]
                ],
                axis=0,
            )
            picked = jnp.dot(pairs, pick_cols, preferred_element_type=f32)
            for e in range(3):
                tap = b * 9 + e * 3
                stage[tap : tap + 3] = picked[:, e * 128 : e * 128 + 128].reshape(3, 4, 8, 128)
        columns = side_by_side([stage[:, q].reshape(216, 128) for q in range(4)]).astype(bf16)
        taps[h] = columns
        part[h] = lax.dot_general(
            w, columns, (((0,), (0,)), ((), ())), preferred_element_type=f32
        ).reshape(16, 8, 512)
        for k in far_first + (0,):
            other = (1 - half) * 8 + lax.rem(place + k, 8)
            z_copies[h, k] = send(
                part.at[h, other], from_z.at[h, k], s_z.at[h, k], r_z.at[h, k], chan=partner
            )

    y_copies = {}
    own = {}
    for h in (1, 0):
        for k in far_first + (0,):
            z_copies[h, k].wait_recv()
            both = part[h, along(k)] + from_z[h, k]
            if k == 0:
                own[h] = both
            else:
                z_sum[h, k] = both
                y_copies[h, k] = send(
                    z_sum.at[h, k], from_y.at[h, k], s_y.at[h, k], r_y.at[h, k], chan=along(k)
                )
    spread = jnp.dot(up[...], pool_picker(), preferred_element_type=f32) * 0.125
    gy, gz = {}, {}
    for h in (1, 0):
        for k in (1, 7, 2, 6, 3, 5, 4):
            y_copies[h, k].wait_recv()
            own[h] = own[h] + from_y[h, k]
        factor = jnp.where(own[h] > 0, 1.0, slope_neg)
        panel[h, chan] = (spread[:, h * 512 : h * 512 + 512] * factor).astype(bf16)
        block = panel.at[h, chan]
        for k in far_first:
            gy[h, k] = send(block, block, s_gy.at[h, k], r_gy.at[h, k], chan=along(k))
        gz[h, 0] = send(block, block, s_gz.at[h, 0], r_gz.at[h, 0], chan=partner)
    for h in (1, 0):
        for k in (1, 7, 2, 6, 3, 5, 4):
            gy[h, k].wait_recv()
            block = panel.at[h, before(k)]
            gz[h, k] = send(block, block, s_gz.at[h, k], r_gz.at[h, k], chan=partner)
    across = (((1,), (1,)), ((), ()))
    total = None
    grads = {}
    for h in (1, 0):
        for k in range(8):
            gz[h, k].wait_recv()
        if h == 0:
            first_plane = send(panel.at[0], rim_panel, s_rim.at[1], r_rim.at[1], space=ahead(n_space - 1))
        grads[h] = panel[h].reshape(128, 512)
        term = lax.dot_general(taps[h], grads[h], across, preferred_element_type=f32)
        total = term if total is None else total + term
    terms[0:27] = total.reshape(27, 8, 128)
    terms[27:32] = jnp.zeros((5, 8, 128), f32)
    rs = []
    for k in range(1, n_space):
        peer = ahead(k)
        rs.append(send(terms.at[peer], got.at[k], s_rs.at[k], r_rs.at[k], space=peer))

    for z in range(2):
        for q in range(4):
            folds[z * 4 + q] = jnp.dot(
                w, grads[z][:, q * 128 : q * 128 + 128], preferred_element_type=f32
            ).reshape(27, 8, 128)
    pre = side_by_side([own[0], own[1]])
    act = jnp.where(pre > 0, pre, slope_neg * pre)
    first = act.astype(bf16)
    rest = act - first.astype(f32)
    second = rest.astype(bf16)
    third = (rest - second.astype(f32)).astype(bf16)
    pick = pool_picker()
    mean = sum(
        lax.dot_general(piece, pick, across, preferred_element_type=f32)
        for piece in (third, second, first)
    )
    pooled[...] = (mean * 0.125).astype(bf16)
    first_plane.wait_recv()
    last = jnp.where(
        space < n_space - 1,
        jnp.dot(w, rim_panel[...].reshape(128, 512), preferred_element_type=f32),
        0.0,
    )
    for q in range(4):
        folds[8 + q] = last[:, q * 128 : q * 128 + 128].reshape(27, 8, 128)
    tall = []
    for b in range(3):
        for a in range(3):
            start = 4 if a == 0 else 0
            tall.append(
                side_by_side(
                    [
                        folds[start : start + 8, b * 9 + e * 3 + a].reshape(64, 128)
                        for e in range(3)
                    ]
                )
            )
    rows = jnp.concatenate(tall, axis=0)
    high = rows.astype(bf16)
    low = (rows - high.astype(f32)).astype(bf16)
    fold = lax.dot_general(high, pick_cols, across, preferred_element_type=f32)
    fold = fold + lax.dot_general(low, pick_cols, across, preferred_element_type=f32)
    fold = fold.reshape(3, 3, 2, 4, 8, 256)
    order = channel_first()
    depth_terms = (((1, 0),), ((2, 0), (0, 0)), ((1, 1),), ((2, 1), (0, 1)))
    for i in range(4):
        by_b = []
        for b in range(3):
            acc = None
            for a, zi in depth_terms[i]:
                acc = fold[b, a, zi] if acc is None else acc + fold[b, a, zi]
            by_b.append(acc)
        back, here, on = by_b
        shifted = jnp.concatenate([back[1:, :, :128], jnp.zeros((1, 8, 128), f32)], axis=0)
        plane = jnp.concatenate(
            [
                here[:, :, :128],
                on[:, :, :128] + back[:, :, 128:],
                here[:, :, 128:],
                on[:, :, 128:] + shifted,
            ],
            axis=0,
        ).reshape(128, 128)
        moved = jnp.dot(order, plane.astype(bf16), preferred_element_type=f32)
        grad_out[:, i] = moved.astype(bf16).reshape(8, 16, 128)

    share = terms[space]
    for k in range(1, n_space):
        rs[k - 1].wait_recv()
        share = share + got[k]
    mine[space] = share
    ag = []
    for k in range(1, n_space):
        block = mine.at[space]
        ag.append(send(block, block, s_ag.at[k], r_ag.at[k], space=ahead(k)))
    for copy in ag:
        copy.wait_recv()
    total_out[...] = mine[...]
    for copy in sent:
        copy.wait_send()


def in_vmem(count):
    return [pl.BlockSpec(memory_space=pltpu.VMEM)] * count


def shaped(*shape, dtype=f32):
    return jax.ShapeDtypeStruct(shape, dtype)


def block(vol, weights, up):
    n = lax.axis_size("space")
    dma = pltpu.SemaphoreType.DMA
    return pl.pallas_call(
        lambda *refs: block_kernel(n, *refs),
        name="block",
        out_shape=(
            shaped(8, 128, dtype=bf16),
            shaped(8, 4, 16, 128, dtype=bf16),
            shaped(n, 8, 128),
        ),
        in_specs=in_vmem(3),
        out_specs=tuple(in_vmem(3)),
        scratch_shapes=[
            pltpu.VMEM((8, 16, 128), bf16),
            pltpu.VMEM((27, 4, 8, 128), f32),
            pltpu.VMEM((2, 216, 512), bf16),
            pltpu.VMEM((2, 16, 8, 512), f32),
            pltpu.VMEM((2, 8, 8, 512), f32),
            pltpu.VMEM((2, 8, 8, 512), f32),
            pltpu.VMEM((2, 8, 8, 512), f32),
            pltpu.VMEM((2, 16, 8, 512), bf16),
            pltpu.VMEM((16, 8, 512), bf16),
            pltpu.VMEM((12, 27, 8, 128), f32),
            pltpu.VMEM((n, 8, 128), f32),
            pltpu.VMEM((n, 8, 128), f32),
            pltpu.VMEM((n, 8, 128), f32),
        ]
        + [dma((2,))] * 2
        + [dma((2, 8))] * 8
        + [dma((n,))] * 4,
        compiler_params=pltpu.CompilerParams(collective_id=0, has_side_effects=True),
    )(vol, weights, up)


def on_device(volume, kernel, upstream):
    weights = kernel.transpose(2, 3, 1, 0, 4).reshape(216, 128)
    pooled, input_grad, total = block(volume, weights, upstream.reshape(8, 128))
    kernel_grad = total[:27].reshape(3, 3, 3, 8, 128).transpose(3, 2, 0, 1, 4)
    return pooled.reshape(upstream.shape), input_grad, kernel_grad


def solution(mesh):
    return jax.shard_map(
        on_device,
        mesh=mesh,
        in_specs=(
            P("chan", "space", None, None),
            P("chan", None, None, None, None),
            P("chan", "space", None, None),
        ),
        out_specs=(
            P("chan", "space", None, None),
            P("chan", "space", None, None),
            P("chan", None, None, None, None),
        ),
        check_vma=False,
    )
```

```python
import jax
import jax.numpy as jnp
from jax import lax
from jax.experimental import pallas as pl
from jax.experimental.pallas import tpu as pltpu
from jax.sharding import PartitionSpec as P

slope_neg = 0.3
MESH = pl.DeviceIdType.MESH
bf16, f32, i32 = jnp.bfloat16, jnp.float32, jnp.int32


def iota(shape, dim):
    return lax.broadcasted_iota(i32, shape, dim)


def one_hot(condition):
    return jnp.where(condition, 1.0, 0.0).astype(bf16)


def row_picker():
    out, inn = iota((160, 128), 0), iota((160, 128), 1)
    same = (out & 7) == (inn >> 4)
    return one_hot(same & ((inn & 15) == 4 * ((out >> 3) & 3) + (out >> 5) - 1))


def column_picker():
    inn, out = iota((256, 384), 0), iota((256, 384), 1)
    same = (inn >> 7) == ((out >> 6) & 1)
    return one_hot(same & ((inn & 127) == 2 * (out & 63) + (out >> 7) - 1))


def pool_picker():
    coarse, fine = iota((128, 1024), 0), iota((128, 1024), 1)
    return one_hot(
        ((coarse >> 5) == ((fine >> 7) & 3)) & ((coarse & 31) == ((fine >> 1) & 31))
    )


def channel_first():
    out, inn = iota((128, 128), 0), iota((128, 128), 1)
    row = 4 * ((inn >> 3) & 3) + (inn >> 5)
    return one_hot(((out >> 4) == (inn & 7)) & ((out & 15) == row))


def side_by_side(blocks):
    return jnp.concatenate(blocks, axis=1)


def block_kernel(
    n_space,
    vol,
    weights,
    up,
    pooled,
    grad_out,
    total_out,
    rim,
    stage,
    taps,
    part,
    from_z,
    z_sum,
    from_y,
    panel,
    rim_panel,
    folds,
    terms,
    got,
    mine,
    s_rim,
    r_rim,
    s_z,
    r_z,
    s_y,
    r_y,
    s_gy,
    r_gy,
    s_gz,
    r_gz,
    s_rs,
    r_rs,
    s_ag,
    r_ag,
):
    space, chan = lax.axis_index("space"), lax.axis_index("chan")
    half = lax.div(chan, 8)
    place = lax.rem(chan, 8)
    partner = lax.rem(chan + 8, 16)

    def along(k):
        return half * 8 + lax.rem(place + k, 8)

    def before(k):
        return half * 8 + lax.rem(place + 8 - k, 8)

    def ahead(k):
        return lax.rem(space + k, n_space)

    sent = []

    def send(src, dst, send_sem, recv_sem, **device):
        copy = pltpu.make_async_remote_copy(
            src_ref=src,
            dst_ref=dst,
            send_sem=send_sem,
            recv_sem=recv_sem,
            device_id=device,
            device_id_type=MESH,
        )
        copy.start()
        sent.append(copy)
        return copy

    barrier = pltpu.get_barrier_semaphore()
    for k in range(1, 8):
        pl.semaphore_signal(barrier, inc=1, device_id={"chan": along(k)}, device_id_type=MESH)
    pl.semaphore_signal(barrier, inc=1, device_id={"chan": partner}, device_id_type=MESH)
    for k in range(1, n_space):
        pl.semaphore_signal(barrier, inc=1, device_id={"space": ahead(k)}, device_id_type=MESH)

    pick_rows = row_picker()
    pick_cols = column_picker()

    def rows_of(plane):
        return jnp.dot(pick_rows, plane.reshape(128, 128), preferred_element_type=f32)

    planes = [None] + [rows_of(vol[:, p]).astype(bf16) for p in range(4)]
    pl.semaphore_wait(barrier, 8 + n_space - 1)
    rim_copy = send(vol.at[:, 3], rim, s_rim.at[0], r_rim.at[0], space=ahead(1))

    far_first = (4, 3, 5, 2, 6, 1, 7)
    w = weights[...]
    z_copies = {}
    for h in (1, 0):
        if h == 0:
            rim_copy.wait_recv()
            planes[0] = jnp.where(space > 0, rows_of(rim[...]), 0.0).astype(bf16)
        for b in range(3):
            pairs = jnp.concatenate(
                [
                    side_by_side([u[32 * b : 32 * b + 32], u[32 * b + 64 : 32 * b + 96]])
                    for u in planes[2 * h : 2 * h + 3]
                ],
                axis=0,
            )
            picked = jnp.dot(pairs, pick_cols, preferred_element_type=f32)
            for e in range(3):
                stage[:, b * 3 + e] = picked[:, e * 128 : e * 128 + 128].reshape(3, 4, 8, 128)
        columns = side_by_side([stage[:, :, q].reshape(216, 128) for q in range(4)]).astype(bf16)
        taps[h] = columns
        part[h] = lax.dot_general(
            w, columns, (((0,), (0,)), ((), ())), preferred_element_type=f32
        ).reshape(16, 8, 512)
        for k in far_first + (0,):
            other = (1 - half) * 8 + lax.rem(place + k, 8)
            z_copies[h, k] = send(
                part.at[h, other], from_z.at[h, k], s_z.at[h, k], r_z.at[h, k], chan=partner
            )

    y_copies = {}
    own = {}
    for h in (1, 0):
        for k in far_first + (0,):
            z_copies[h, k].wait_recv()
            both = part[h, along(k)] + from_z[h, k]
            if k == 0:
                own[h] = both
            else:
                z_sum[h, k] = both
                y_copies[h, k] = send(
                    z_sum.at[h, k], from_y.at[h, k], s_y.at[h, k], r_y.at[h, k], chan=along(k)
                )
    coarse = up[...].astype(f32).reshape(8, 4, 32)
    flat = side_by_side([coarse[:, q] for q in range(4)]).astype(bf16)
    spread = jnp.dot(flat, pool_picker(), preferred_element_type=f32) * 0.125
    gy, gz = {}, {}
    for h in (1, 0):
        for k in (1, 7, 2, 6, 3, 5, 4):
            y_copies[h, k].wait_recv()
            own[h] = own[h] + from_y[h, k]
        factor = jnp.where(own[h] > 0, 1.0, slope_neg)
        panel[h, chan] = (spread[:, h * 512 : h * 512 + 512] * factor).astype(bf16)
        block = panel.at[h, chan]
        for k in far_first:
            gy[h, k] = send(block, block, s_gy.at[h, k], r_gy.at[h, k], chan=along(k))
        gz[h, 0] = send(block, block, s_gz.at[h, 0], r_gz.at[h, 0], chan=partner)
    for h in (1, 0):
        for k in (1, 7, 2, 6, 3, 5, 4):
            gy[h, k].wait_recv()
            block = panel.at[h, before(k)]
            gz[h, k] = send(block, block, s_gz.at[h, k], r_gz.at[h, k], chan=partner)
    across = (((1,), (1,)), ((), ()))
    total = None
    grads = {}
    for h in (1, 0):
        for k in range(8):
            gz[h, k].wait_recv()
        if h == 0:
            first_plane = send(panel.at[0], rim_panel, s_rim.at[1], r_rim.at[1], space=ahead(n_space - 1))
        grads[h] = panel[h].reshape(128, 512)
        term = lax.dot_general(taps[h], grads[h], across, preferred_element_type=f32)
        total = term if total is None else total + term
    terms[0:27] = total.reshape(27, 8, 128)
    terms[27:32] = jnp.zeros((5, 8, 128), f32)
    rs = []
    for k in range(1, n_space):
        peer = ahead(k)
        rs.append(send(terms.at[peer], got.at[k], s_rs.at[k], r_rs.at[k], space=peer))

    for z in range(2):
        for q in range(4):
            folds[z * 4 + q] = jnp.dot(
                w, grads[z][:, q * 128 : q * 128 + 128], preferred_element_type=f32
            ).reshape(27, 8, 128)
    pre = side_by_side([own[0], own[1]])
    act = jnp.where(pre > 0, pre, slope_neg * pre)
    first = act.astype(bf16)
    rest = act - first.astype(f32)
    second = rest.astype(bf16)
    third = (rest - second.astype(f32)).astype(bf16)
    pick = pool_picker()
    mean = sum(
        lax.dot_general(piece, pick, across, preferred_element_type=f32)
        for piece in (third, second, first)
    )
    mean = jnp.stack([mean[:, q * 32 : q * 32 + 32] for q in range(4)], axis=1)
    pooled[...] = (mean * 0.125).astype(bf16).reshape(8, 1, 4, 32)
    first_plane.wait_recv()
    last = jnp.where(
        space < n_space - 1,
        jnp.dot(w, rim_panel[...].reshape(128, 512), preferred_element_type=f32),
        0.0,
    )
    for q in range(4):
        folds[8 + q] = last[:, q * 128 : q * 128 + 128].reshape(27, 8, 128)
    tall = []
    for b in range(3):
        for a in range(3):
            start = 4 if a == 0 else 0
            tall.append(
                side_by_side(
                    [
                        folds[start : start + 8, a * 9 + b * 3 + e].reshape(64, 128)
                        for e in range(3)
                    ]
                )
            )
    rows = jnp.concatenate(tall, axis=0)
    high = rows.astype(bf16)
    low = (rows - high.astype(f32)).astype(bf16)
    fold = lax.dot_general(high, pick_cols, across, preferred_element_type=f32)
    fold = fold + lax.dot_general(low, pick_cols, across, preferred_element_type=f32)
    fold = fold.reshape(3, 3, 2, 4, 8, 256)
    order = channel_first()
    depth_terms = (((1, 0),), ((2, 0), (0, 0)), ((1, 1),), ((2, 1), (0, 1)))
    for i in range(4):
        by_b = []
        for b in range(3):
            acc = None
            for a, zi in depth_terms[i]:
                acc = fold[b, a, zi] if acc is None else acc + fold[b, a, zi]
            by_b.append(acc)
        back, here, on = by_b
        shifted = jnp.concatenate([back[1:, :, :128], jnp.zeros((1, 8, 128), f32)], axis=0)
        plane = jnp.concatenate(
            [
                here[:, :, :128],
                on[:, :, :128] + back[:, :, 128:],
                here[:, :, 128:],
                on[:, :, 128:] + shifted,
            ],
            axis=0,
        ).reshape(128, 128)
        moved = jnp.dot(order, plane.astype(bf16), preferred_element_type=f32)
        grad_out[:, i] = moved.astype(bf16).reshape(8, 16, 128)

    share = terms[space]
    for k in range(1, n_space):
        rs[k - 1].wait_recv()
        share = share + got[k]
    mine[space] = share
    ag = []
    for k in range(1, n_space):
        block = mine.at[space]
        ag.append(send(block, block, s_ag.at[k], r_ag.at[k], space=ahead(k)))
    for copy in ag:
        copy.wait_recv()
    total_out[...] = mine[0:27]
    for copy in sent:
        copy.wait_send()


def in_vmem(count):
    return [pl.BlockSpec(memory_space=pltpu.VMEM)] * count


def shaped(*shape, dtype=f32):
    return jax.ShapeDtypeStruct(shape, dtype)


def block(vol, weights, up):
    n = lax.axis_size("space")
    dma = pltpu.SemaphoreType.DMA
    return pl.pallas_call(
        lambda *refs: block_kernel(n, *refs),
        name="block",
        out_shape=(
            shaped(8, 1, 4, 32, dtype=bf16),
            shaped(8, 4, 16, 128, dtype=bf16),
            shaped(27, 8, 128),
        ),
        in_specs=in_vmem(3),
        out_specs=tuple(in_vmem(3)),
        scratch_shapes=[
            pltpu.VMEM((8, 16, 128), bf16),
            pltpu.VMEM((3, 9, 4, 8, 128), f32),
            pltpu.VMEM((2, 216, 512), bf16),
            pltpu.VMEM((2, 16, 8, 512), f32),
            pltpu.VMEM((2, 8, 8, 512), f32),
            pltpu.VMEM((2, 8, 8, 512), f32),
            pltpu.VMEM((2, 8, 8, 512), f32),
            pltpu.VMEM((2, 16, 8, 512), bf16),
            pltpu.VMEM((16, 8, 512), bf16),
            pltpu.VMEM((12, 27, 8, 128), f32),
            pltpu.VMEM((n, 8, 128), f32),
            pltpu.VMEM((n, 8, 128), f32),
            pltpu.VMEM((n, 8, 128), f32),
        ]
        + [dma((2,))] * 2
        + [dma((2, 8))] * 8
        + [dma((n,))] * 4,
        compiler_params=pltpu.CompilerParams(collective_id=0, has_side_effects=True),
    )(vol, weights, up)


def on_device(volume, kernel, upstream):
    weights = kernel.transpose(1, 2, 3, 0, 4).reshape(216, 128)
    pooled, input_grad, total = block(volume, weights, upstream)
    kernel_grad = total.reshape(3, 3, 3, 8, 128).transpose(3, 0, 1, 2, 4)
    return pooled, input_grad, kernel_grad


def solution(mesh):
    return jax.shard_map(
        on_device,
        mesh=mesh,
        in_specs=(
            P("chan", "space", None, None),
            P("chan", None, None, None, None),
            P("chan", "space", None, None),
        ),
        out_specs=(
            P("chan", "space", None, None),
            P("chan", "space", None, None),
            P("chan", None, None, None, None),
        ),
        check_vma=False,
    )
```

```python
import jax
import jax.numpy as jnp
from jax import lax
from jax.experimental import pallas as pl
from jax.experimental.pallas import tpu as pltpu
from jax.sharding import PartitionSpec as P

slope_neg = 0.3
MESH = pl.DeviceIdType.MESH
bf16, f32, i32 = jnp.bfloat16, jnp.float32, jnp.int32


def iota(shape, dim):
    return lax.broadcasted_iota(i32, shape, dim)


def one_hot(condition):
    return jnp.where(condition, 1.0, 0.0).astype(bf16)


def row_picker():
    out, inn = iota((160, 128), 0), iota((160, 128), 1)
    same = (out & 7) == (inn >> 4)
    return one_hot(same & ((inn & 15) == 4 * ((out >> 3) & 3) + (out >> 5) - 1))


def column_picker():
    inn, out = iota((256, 384), 0), iota((256, 384), 1)
    same = (inn >> 7) == ((out >> 6) & 1)
    return one_hot(same & ((inn & 127) == 2 * (out & 63) + (out >> 7) - 1))


def pool_picker():
    coarse, fine = iota((128, 1024), 0), iota((128, 1024), 1)
    return one_hot(
        ((coarse >> 5) == ((fine >> 7) & 3)) & ((coarse & 31) == ((fine >> 1) & 31))
    )


def channel_first():
    out, inn = iota((128, 128), 0), iota((128, 128), 1)
    row = 4 * ((inn >> 3) & 3) + (inn >> 5)
    return one_hot(((out >> 4) == (inn & 7)) & ((out & 15) == row))


def side_by_side(blocks):
    return jnp.concatenate(blocks, axis=1)


def block_kernel(
    n_space,
    vol,
    weights,
    up,
    pooled,
    grad_out,
    total_out,
    rim,
    spread,
    stage,
    taps,
    part,
    from_z,
    z_sum,
    from_y,
    panel,
    rim_panel,
    folds,
    terms,
    got,
    mine,
    s_rim,
    r_rim,
    s_z,
    r_z,
    s_y,
    r_y,
    s_gy,
    r_gy,
    s_gz,
    r_gz,
    s_rs,
    r_rs,
    s_up,
    r_up,
    s_ag,
    r_ag,
):
    space, chan = lax.axis_index("space"), lax.axis_index("chan")
    half = lax.div(chan, 8)
    place = lax.rem(chan, 8)
    partner = lax.rem(chan + 8, 16)

    def along(k):
        return half * 8 + lax.rem(place + k, 8)

    def opposite(k):
        return (1 - half) * 8 + lax.rem(place + k, 8)

    def before(k):
        return half * 8 + lax.rem(place + 8 - k, 8)

    def ahead(k):
        return lax.rem(space + k, n_space)

    sent = []

    def send(src, dst, send_sem, recv_sem, **device):
        copy = pltpu.make_async_remote_copy(
            src_ref=src,
            dst_ref=dst,
            send_sem=send_sem,
            recv_sem=recv_sem,
            device_id=device,
            device_id_type=MESH,
        )
        copy.start()
        sent.append(copy)
        return copy

    barrier = pltpu.get_barrier_semaphore()
    for k in range(1, 8):
        pl.semaphore_signal(barrier, inc=1, device_id={"chan": along(k)}, device_id_type=MESH)
    for k in (0, 3, 4, 5):
        pl.semaphore_signal(barrier, inc=1, device_id={"chan": opposite(k)}, device_id_type=MESH)
    for k in range(1, n_space):
        pl.semaphore_signal(barrier, inc=1, device_id={"space": ahead(k)}, device_id_type=MESH)

    pick_rows = row_picker()
    pick_cols = column_picker()

    def rows_of(plane):
        return jnp.dot(pick_rows, plane.reshape(128, 128), preferred_element_type=f32)

    planes = [None] + [rows_of(vol[:, p]).astype(bf16) for p in range(4)]
    w = weights[...]

    def fill(used, first):
        count = len(used)
        for b in range(3):
            pairs = jnp.concatenate(
                [
                    side_by_side([u[32 * b : 32 * b + 32], u[32 * b + 64 : 32 * b + 96]])
                    for u in used
                ],
                axis=0,
            )
            picked = jnp.dot(pairs, pick_cols, preferred_element_type=f32)
            for e in range(3):
                stage[first : first + count, b * 3 + e] = picked[
                    :, e * 128 : e * 128 + 128
                ].reshape(count, 4, 8, 128)

    def multiply(h):
        columns = side_by_side([stage[:, :, q].reshape(216, 128) for q in range(4)]).astype(bf16)
        taps[h] = columns
        part[h] = lax.dot_general(
            w, columns, (((0,), (0,)), ((), ())), preferred_element_type=f32
        ).reshape(16, 8, 512)

    far_first = (4, 3, 5, 2, 6, 1, 7)
    z_copies = {}

    def send_half(h):
        for k in far_first + (0,):
            z_copies[h, k] = send(
                part.at[h, opposite(k)], from_z.at[h, k], s_z.at[h, k], r_z.at[h, k], chan=partner
            )

    fill(planes[2:5], 0)
    multiply(1)
    fill(planes[1:3], 1)
    coarse = up[...].astype(f32).reshape(8, 4, 32)
    flat = side_by_side([coarse[:, q] for q in range(4)]).astype(bf16)
    spread[...] = jnp.dot(flat, pool_picker(), preferred_element_type=f32) * 0.125
    pl.semaphore_wait(barrier, 7 + 4 + n_space - 1)
    rim_copy = send(vol.at[:, 3], rim, s_rim.at[0], r_rim.at[0], space=ahead(1))
    send_half(1)
    rim_copy.wait_recv()
    fill([jnp.where(space > 0, rows_of(rim[...]), 0.0).astype(bf16)], 0)
    multiply(0)
    send_half(0)

    y_copies = {}
    own = {}
    for h in (1, 0):
        for k in far_first + (0,):
            z_copies[h, k].wait_recv()
            both = part[h, along(k)] + from_z[h, k]
            if k == 0:
                own[h] = both
            else:
                z_sum[h, k] = both
                y_copies[h, k] = send(
                    z_sum.at[h, k], from_y.at[h, k], s_y.at[h, k], r_y.at[h, k], chan=along(k)
                )
    gy, gz = {}, {}
    for h in (1, 0):
        for k in (1, 7, 2, 6, 3, 5, 4):
            y_copies[h, k].wait_recv()
            own[h] = own[h] + from_y[h, k]
        factor = jnp.where(own[h] > 0, 1.0, slope_neg)
        panel[h, chan] = (spread[:, h * 512 : h * 512 + 512] * factor).astype(bf16)
        block = panel.at[h, chan]
        for k in far_first:
            gy[h, k] = send(block, block, s_gy.at[h, k], r_gy.at[h, k], chan=along(k))
        for k in (4, 3, 5, 0):
            gz[h, k] = send(block, block, s_gz.at[h, k], r_gz.at[h, k], chan=opposite(k))
    for h in (1, 0):
        for k in (1, 7, 2, 6):
            gy[h, k].wait_recv()
            block = panel.at[h, before(k)]
            gz[h, k] = send(block, block, s_gz.at[h, k], r_gz.at[h, k], chan=partner)
    across = (((1,), (1,)), ((), ()))
    total = None
    grads = {}
    for h in (1, 0):
        for k in (3, 5, 4):
            gy[h, k].wait_recv()
        for k in range(8):
            gz[h, k].wait_recv()
        if h == 0:
            first_plane = send(panel.at[0], rim_panel, s_rim.at[1], r_rim.at[1], space=ahead(n_space - 1))
        grads[h] = panel[h].reshape(128, 512)
        term = lax.dot_general(taps[h], grads[h], across, preferred_element_type=f32)
        total = term if total is None else total + term
    terms[0:27] = total.reshape(27, 8, 128)
    terms[27:32] = jnp.zeros((5, 8, 128), f32)
    rs = []
    for k in range(1, n_space):
        peer = ahead(k)
        rs.append(send(terms.at[peer], got.at[k], s_rs.at[k], r_rs.at[k], space=peer))

    for z in range(2):
        for q in range(4):
            folds[z * 4 + q] = jnp.dot(
                w, grads[z][:, q * 128 : q * 128 + 128], preferred_element_type=f32
            ).reshape(27, 8, 128)
    pre = side_by_side([own[0], own[1]])
    act = jnp.where(pre > 0, pre, slope_neg * pre)
    first = act.astype(bf16)
    rest = act - first.astype(f32)
    second = rest.astype(bf16)
    third = (rest - second.astype(f32)).astype(bf16)
    pick = pool_picker()
    mean = sum(
        lax.dot_general(piece, pick, across, preferred_element_type=f32)
        for piece in (third, second, first)
    )
    mean = jnp.stack([mean[:, q * 32 : q * 32 + 32] for q in range(4)], axis=1)
    pooled[...] = (mean * 0.125).astype(bf16).reshape(8, 1, 4, 32)
    first_plane.wait_recv()
    last = jnp.where(
        space < n_space - 1,
        jnp.dot(w, rim_panel[...].reshape(128, 512), preferred_element_type=f32),
        0.0,
    )
    for q in range(4):
        folds[8 + q] = last[:, q * 128 : q * 128 + 128].reshape(27, 8, 128)
    tall = []
    for b in range(3):
        for a in range(3):
            start = 4 if a == 0 else 0
            tall.append(
                side_by_side(
                    [
                        folds[start : start + 8, a * 9 + b * 3 + e].reshape(64, 128)
                        for e in range(3)
                    ]
                )
            )
    rows = jnp.concatenate(tall, axis=0)
    high = rows.astype(bf16)
    low = (rows - high.astype(f32)).astype(bf16)
    fold = lax.dot_general(high, pick_cols, across, preferred_element_type=f32)
    fold = fold + lax.dot_general(low, pick_cols, across, preferred_element_type=f32)
    fold = fold.reshape(3, 3, 2, 4, 8, 256)
    order = channel_first()
    depth_terms = (((1, 0),), ((2, 0), (0, 0)), ((1, 1),), ((2, 1), (0, 1)))
    for i in range(4):
        by_b = []
        for b in range(3):
            acc = None
            for a, zi in depth_terms[i]:
                acc = fold[b, a, zi] if acc is None else acc + fold[b, a, zi]
            by_b.append(acc)
        back, here, on = by_b
        shifted = jnp.concatenate([back[1:, :, :128], jnp.zeros((1, 8, 128), f32)], axis=0)
        plane = jnp.concatenate(
            [
                here[:, :, :128],
                on[:, :, :128] + back[:, :, 128:],
                here[:, :, 128:],
                on[:, :, 128:] + shifted,
            ],
            axis=0,
        ).reshape(128, 128)
        moved = jnp.dot(order, plane.astype(bf16), preferred_element_type=f32)
        grad_out[:, i] = moved.astype(bf16).reshape(8, 16, 128)

    share = terms[space]
    for k in range(1, n_space):
        rs[k - 1].wait_recv()
        share = share + got[k]
    mine[space] = share
    layers = n_space // 8
    layer = lax.div(space, 8)
    slot = lax.rem(space, 8)
    hops = {}
    for k in range(1, layers):
        block = mine.at[space]
        hops[k] = send(block, block, s_up.at[k], r_up.at[k], space=lax.rem(space + 8 * k, n_space))
    spreads = []
    for k in range(layers):
        if k > 0:
            hops[k].wait_recv()
        block = mine.at[lax.rem(space + n_space - 8 * k, n_space)]
        for m in range(1, 8):
            peer = layer * 8 + lax.rem(slot + m, 8)
            spreads.append(send(block, block, s_ag.at[k, m], r_ag.at[k, m], space=peer))
    for copy in spreads:
        copy.wait_recv()
    total_out[...] = mine[0:27]
    for copy in sent:
        copy.wait_send()


def in_vmem(count):
    return [pl.BlockSpec(memory_space=pltpu.VMEM)] * count


def shaped(*shape, dtype=f32):
    return jax.ShapeDtypeStruct(shape, dtype)


def block(vol, weights, up):
    n = lax.axis_size("space")
    dma = pltpu.SemaphoreType.DMA
    return pl.pallas_call(
        lambda *refs: block_kernel(n, *refs),
        name="block",
        out_shape=(
            shaped(8, 1, 4, 32, dtype=bf16),
            shaped(8, 4, 16, 128, dtype=bf16),
            shaped(27, 8, 128),
        ),
        in_specs=in_vmem(3),
        out_specs=tuple(in_vmem(3)),
        scratch_shapes=[
            pltpu.VMEM((8, 16, 128), bf16),
            pltpu.VMEM((8, 1024), f32),
            pltpu.VMEM((3, 9, 4, 8, 128), f32),
            pltpu.VMEM((2, 216, 512), bf16),
            pltpu.VMEM((2, 16, 8, 512), f32),
            pltpu.VMEM((2, 8, 8, 512), f32),
            pltpu.VMEM((2, 8, 8, 512), f32),
            pltpu.VMEM((2, 8, 8, 512), f32),
            pltpu.VMEM((2, 16, 8, 512), bf16),
            pltpu.VMEM((16, 8, 512), bf16),
            pltpu.VMEM((12, 27, 8, 128), f32),
            pltpu.VMEM((n, 8, 128), f32),
            pltpu.VMEM((n, 8, 128), f32),
            pltpu.VMEM((n, 8, 128), f32),
        ]
        + [dma((2,))] * 2
        + [dma((2, 8))] * 8
        + [dma((n,))] * 2
        + [dma((n // 8,))] * 2
        + [dma((n // 8, 8))] * 2,
        compiler_params=pltpu.CompilerParams(collective_id=0, has_side_effects=True),
    )(vol, weights, up)


def hand_over(*arrays):
    def kernel(*refs):
        for source, target in zip(refs[:3], refs[3:]):
            target[...] = source[...]

    return pl.pallas_call(
        kernel,
        name="hand_over",
        out_shape=tuple(jax.ShapeDtypeStruct(x.shape, x.dtype) for x in arrays),
        in_specs=in_vmem(3),
        out_specs=tuple(in_vmem(3)),
    )(*arrays)


def on_device(volume, kernel, upstream):
    weights = kernel.transpose(1, 2, 3, 0, 4).reshape(216, 128)
    pooled, input_grad, total = hand_over(*block(volume, weights, upstream))
    kernel_grad = total.reshape(3, 3, 3, 8, 128).transpose(3, 0, 1, 2, 4)
    return pooled, input_grad, kernel_grad


def solution(mesh):
    return jax.shard_map(
        on_device,
        mesh=mesh,
        in_specs=(
            P("chan", "space", None, None),
            P("chan", None, None, None, None),
            P("chan", "space", None, None),
        ),
        out_specs=(
            P("chan", "space", None, None),
            P("chan", "space", None, None),
            P("chan", None, None, None, None),
        ),
        check_vma=False,
    )
```

```python
import jax
import jax.numpy as jnp
from jax import lax
from jax.experimental import pallas as pl
from jax.experimental.pallas import tpu as pltpu
from jax.sharding import PartitionSpec as P

slope_neg = 0.3
MESH = pl.DeviceIdType.MESH
bf16, f32, i32 = jnp.bfloat16, jnp.float32, jnp.int32


def iota(shape, dim):
    return lax.broadcasted_iota(i32, shape, dim)


def one_hot(condition):
    return jnp.where(condition, 1.0, 0.0).astype(bf16)


def row_picker():
    out, inn = iota((160, 128), 0), iota((160, 128), 1)
    same = (out & 7) == (inn >> 4)
    return one_hot(same & ((inn & 15) == 4 * ((out >> 3) & 3) + (out >> 5) - 1))


def column_picker():
    inn, out = iota((256, 384), 0), iota((256, 384), 1)
    same = (inn >> 7) == ((out >> 6) & 1)
    return one_hot(same & ((inn & 127) == 2 * (out & 63) + (out >> 7) - 1))


def pool_picker():
    coarse, fine = iota((128, 1024), 0), iota((128, 1024), 1)
    return one_hot(
        ((coarse >> 5) == ((fine >> 7) & 3)) & ((coarse & 31) == ((fine >> 1) & 31))
    )


def channel_first():
    out, inn = iota((128, 128), 0), iota((128, 128), 1)
    row = 4 * ((inn >> 3) & 3) + (inn >> 5)
    return one_hot(((out >> 4) == (inn & 7)) & ((out & 15) == row))


def side_by_side(blocks):
    return jnp.concatenate(blocks, axis=1)


def block_kernel(
    n_space,
    vol,
    weights,
    up,
    pooled,
    grad_out,
    total_out,
    rim,
    spread,
    stage,
    taps,
    part,
    from_z,
    z_sum,
    from_y,
    panel,
    rim_panel,
    folds,
    terms,
    got,
    layer_sums,
    mine,
    s_rim,
    r_rim,
    s_z,
    r_z,
    s_y,
    r_y,
    s_gy,
    r_gy,
    s_gz,
    r_gz,
    s_rs,
    r_rs,
    s_up,
    r_up,
    s_ag,
    r_ag,
):
    space, chan = lax.axis_index("space"), lax.axis_index("chan")
    half = lax.div(chan, 8)
    place = lax.rem(chan, 8)
    partner = lax.rem(chan + 8, 16)

    def along(k):
        return half * 8 + lax.rem(place + k, 8)

    def opposite(k):
        return (1 - half) * 8 + lax.rem(place + k, 8)

    def before(k):
        return half * 8 + lax.rem(place + 8 - k, 8)

    def ahead(k):
        return lax.rem(space + k, n_space)

    sent = []

    def send(src, dst, send_sem, recv_sem, **device):
        copy = pltpu.make_async_remote_copy(
            src_ref=src,
            dst_ref=dst,
            send_sem=send_sem,
            recv_sem=recv_sem,
            device_id=device,
            device_id_type=MESH,
        )
        copy.start()
        sent.append(copy)
        return copy

    barrier = pltpu.get_barrier_semaphore()
    for k in range(1, 8):
        pl.semaphore_signal(barrier, inc=1, device_id={"chan": along(k)}, device_id_type=MESH)
    for k in (0, 3, 4, 5):
        pl.semaphore_signal(barrier, inc=1, device_id={"chan": opposite(k)}, device_id_type=MESH)
    layers = n_space // 8
    layer = lax.div(space, 8)
    slot = lax.rem(space, 8)

    def beside(m):
        return lax.rem(slot + m, 8)

    for m in range(1, 8):
        peer = layer * 8 + beside(m)
        pl.semaphore_signal(barrier, inc=1, device_id={"space": peer}, device_id_type=MESH)
    for k in [8 * k for k in range(1, layers)] + [1, n_space - 1]:
        pl.semaphore_signal(barrier, inc=1, device_id={"space": ahead(k)}, device_id_type=MESH)

    pick_rows = row_picker()
    pick_cols = column_picker()

    def rows_of(plane):
        return jnp.dot(pick_rows, plane.reshape(128, 128), preferred_element_type=f32)

    planes = [None] + [rows_of(vol[:, p]).astype(bf16) for p in range(4)]
    w = weights[...]

    def fill(used, first):
        count = len(used)
        for b in range(3):
            pairs = jnp.concatenate(
                [
                    side_by_side([u[32 * b : 32 * b + 32], u[32 * b + 64 : 32 * b + 96]])
                    for u in used
                ],
                axis=0,
            )
            picked = jnp.dot(pairs, pick_cols, preferred_element_type=f32)
            for e in range(3):
                stage[first : first + count, b * 3 + e] = picked[
                    :, e * 128 : e * 128 + 128
                ].reshape(count, 4, 8, 128)

    def columns_of(count):
        return side_by_side(
            [stage[0:count, :, q].reshape(72 * count, 128) for q in range(4)]
        ).astype(bf16)

    def multiply(rows, columns):
        return lax.dot_general(
            rows, columns, (((0,), (0,)), ((), ())), preferred_element_type=f32
        ).reshape(16, 8, 512)

    far_first = (4, 3, 5, 2, 6, 1, 7)
    z_copies = {}

    def send_half(h):
        for k in far_first + (0,):
            z_copies[h, k] = send(
                part.at[h, opposite(k)], from_z.at[h, k], s_z.at[h, k], r_z.at[h, k], chan=partner
            )

    fill(planes[2:5], 0)
    columns = columns_of(3)
    taps[1] = columns
    part[1] = multiply(w, columns)
    stage[0:1] = jnp.zeros((1, 9, 4, 8, 128), f32)
    fill(planes[1:3], 1)
    part[0] = multiply(w, columns_of(3))
    w_rim = w[0:72]
    coarse = up[...].astype(f32).reshape(8, 4, 32)
    flat = side_by_side([coarse[:, q] for q in range(4)]).astype(bf16)
    spread[...] = jnp.dot(flat, pool_picker(), preferred_element_type=f32) * 0.125
    pl.semaphore_wait(barrier, 7 + 4 + 7 + layers - 1 + 2)
    rim_copy = send(vol.at[:, 3], rim, s_rim.at[0], r_rim.at[0], space=ahead(1))
    send_half(1)
    rim_copy.wait_recv()
    fill([jnp.where(space > 0, rows_of(rim[...]), 0.0).astype(bf16)], 0)
    part[0] = part[0] + multiply(w_rim, columns_of(1))
    send_half(0)
    taps[0] = columns_of(3)

    y_copies = {}
    own = {}
    for h in (1, 0):
        for k in far_first + (0,):
            z_copies[h, k].wait_recv()
            both = part[h, along(k)] + from_z[h, k]
            if k == 0:
                own[h] = both
            else:
                z_sum[h, k] = both
                y_copies[h, k] = send(
                    z_sum.at[h, k], from_y.at[h, k], s_y.at[h, k], r_y.at[h, k], chan=along(k)
                )
    gy, gz = {}, {}
    for h in (1, 0):
        for k in (1, 7, 2, 6, 3, 5, 4):
            y_copies[h, k].wait_recv()
            own[h] = own[h] + from_y[h, k]
        factor = jnp.where(own[h] > 0, 1.0, slope_neg)
        panel[h, chan] = (spread[:, h * 512 : h * 512 + 512] * factor).astype(bf16)
        block = panel.at[h, chan]
        for k in far_first:
            gy[h, k] = send(block, block, s_gy.at[h, k], r_gy.at[h, k], chan=along(k))
        for k in (4, 3, 5, 0):
            gz[h, k] = send(block, block, s_gz.at[h, k], r_gz.at[h, k], chan=opposite(k))
    for h in (1, 0):
        for k in (1, 7, 2, 6):
            gy[h, k].wait_recv()
            block = panel.at[h, before(k)]
            gz[h, k] = send(block, block, s_gz.at[h, k], r_gz.at[h, k], chan=partner)
    across = (((1,), (1,)), ((), ()))
    total = None
    grads = {}
    for h in (1, 0):
        for k in (3, 5, 4):
            gy[h, k].wait_recv()
        for k in range(8):
            gz[h, k].wait_recv()
        if h == 0:
            first_plane = send(panel.at[0], rim_panel, s_rim.at[1], r_rim.at[1], space=ahead(n_space - 1))
        grads[h] = panel[h].reshape(128, 512)
        term = lax.dot_general(taps[h], grads[h], across, preferred_element_type=f32)
        total = term if total is None else total + term
    terms[...] = jnp.concatenate([total, jnp.zeros((40, 128), f32)], axis=0).reshape(8, 32, 128)
    rs = []
    for m in (3, 4, 5, 2, 6, 1, 7):
        peer = layer * 8 + beside(m)
        rs.append(send(terms.at[beside(m)], got.at[m], s_rs.at[m], r_rs.at[m], space=peer))

    for z in range(2):
        for q in range(4):
            folds[z * 4 + q] = jnp.dot(
                w, grads[z][:, q * 128 : q * 128 + 128], preferred_element_type=f32
            ).reshape(27, 8, 128)
    pre = side_by_side([own[0], own[1]])
    act = jnp.where(pre > 0, pre, slope_neg * pre)
    first = act.astype(bf16)
    rest = act - first.astype(f32)
    second = rest.astype(bf16)
    third = (rest - second.astype(f32)).astype(bf16)
    pick = pool_picker()
    mean = sum(
        lax.dot_general(piece, pick, across, preferred_element_type=f32)
        for piece in (third, second, first)
    )
    mean = jnp.stack([mean[:, q * 32 : q * 32 + 32] for q in range(4)], axis=1)
    pooled[...] = (mean * 0.125).astype(bf16).reshape(8, 1, 4, 32)
    share = terms[slot]
    for copy in rs:
        copy.wait_recv()
    for m in range(1, 8):
        share = share + got[m]
    layer_sums[layer] = share
    ups = []
    for k in range(1, layers):
        block = layer_sums.at[layer]
        ups.append(send(block, block, s_up.at[k], r_up.at[k], space=ahead(8 * k)))
    first_plane.wait_recv()
    last = jnp.where(
        space < n_space - 1,
        jnp.dot(w, rim_panel[...].reshape(128, 512), preferred_element_type=f32),
        0.0,
    )
    for q in range(4):
        folds[8 + q] = last[:, q * 128 : q * 128 + 128].reshape(27, 8, 128)
    tall = []
    for b in range(3):
        for a in range(3):
            start = 4 if a == 0 else 0
            tall.append(
                side_by_side(
                    [
                        folds[start : start + 8, a * 9 + b * 3 + e].reshape(64, 128)
                        for e in range(3)
                    ]
                )
            )
    rows = jnp.concatenate(tall, axis=0)
    high = rows.astype(bf16)
    low = (rows - high.astype(f32)).astype(bf16)
    fold = lax.dot_general(high, pick_cols, across, preferred_element_type=f32)
    fold = fold + lax.dot_general(low, pick_cols, across, preferred_element_type=f32)
    for copy in ups:
        copy.wait_recv()
    share = layer_sums[0]
    for k in range(1, layers):
        share = share + layer_sums[k]
    mine[slot] = share
    ag = []
    for m in (3, 4, 5, 2, 6, 1, 7):
        block = mine.at[slot]
        ag.append(send(block, block, s_ag.at[m], r_ag.at[m], space=layer * 8 + beside(m)))
    fold = fold.reshape(3, 3, 2, 4, 8, 256)
    order = channel_first()
    depth_terms = (((1, 0),), ((2, 0), (0, 0)), ((1, 1),), ((2, 1), (0, 1)))
    for i in range(4):
        by_b = []
        for b in range(3):
            acc = None
            for a, zi in depth_terms[i]:
                acc = fold[b, a, zi] if acc is None else acc + fold[b, a, zi]
            by_b.append(acc)
        back, here, on = by_b
        shifted = jnp.concatenate([back[1:, :, :128], jnp.zeros((1, 8, 128), f32)], axis=0)
        plane = jnp.concatenate(
            [
                here[:, :, :128],
                on[:, :, :128] + back[:, :, 128:],
                here[:, :, 128:],
                on[:, :, 128:] + shifted,
            ],
            axis=0,
        ).reshape(128, 128)
        moved = jnp.dot(order, plane.astype(bf16), preferred_element_type=f32)
        grad_out[:, i] = moved.astype(bf16).reshape(8, 16, 128)

    for copy in ag:
        copy.wait_recv()
    for m in range(7):
        total_out[4 * m : min(4 * m + 4, 27)] = mine[m].reshape(4, 8, 128)[: min(4, 27 - 4 * m)]
    for copy in sent:
        copy.wait_send()


def in_vmem(count):
    return [pl.BlockSpec(memory_space=pltpu.VMEM)] * count


def shaped(*shape, dtype=f32):
    return jax.ShapeDtypeStruct(shape, dtype)


def block(vol, weights, up):
    n = lax.axis_size("space")
    dma = pltpu.SemaphoreType.DMA
    return pl.pallas_call(
        lambda *refs: block_kernel(n, *refs),
        name="block",
        out_shape=(
            shaped(8, 1, 4, 32, dtype=bf16),
            shaped(8, 4, 16, 128, dtype=bf16),
            shaped(27, 8, 128),
        ),
        in_specs=in_vmem(3),
        out_specs=tuple(in_vmem(3)),
        scratch_shapes=[
            pltpu.VMEM((8, 16, 128), bf16),
            pltpu.VMEM((8, 1024), f32),
            pltpu.VMEM((3, 9, 4, 8, 128), f32),
            pltpu.VMEM((2, 216, 512), bf16),
            pltpu.VMEM((2, 16, 8, 512), f32),
            pltpu.VMEM((2, 8, 8, 512), f32),
            pltpu.VMEM((2, 8, 8, 512), f32),
            pltpu.VMEM((2, 8, 8, 512), f32),
            pltpu.VMEM((2, 16, 8, 512), bf16),
            pltpu.VMEM((16, 8, 512), bf16),
            pltpu.VMEM((12, 27, 8, 128), f32),
            pltpu.VMEM((8, 32, 128), f32),
            pltpu.VMEM((8, 32, 128), f32),
            pltpu.VMEM((n // 8, 32, 128), f32),
            pltpu.VMEM((8, 32, 128), f32),
        ]
        + [dma((2,))] * 2
        + [dma((2, 8))] * 8
        + [dma((8,))] * 2
        + [dma((n // 8,))] * 2
        + [dma((8,))] * 2,
        compiler_params=pltpu.CompilerParams(collective_id=0, has_side_effects=True),
    )(vol, weights, up)


def hand_over(*arrays):
    def kernel(*refs):
        for source, target in zip(refs[:3], refs[3:]):
            target[...] = source[...]

    return pl.pallas_call(
        kernel,
        name="hand_over",
        out_shape=tuple(jax.ShapeDtypeStruct(x.shape, x.dtype) for x in arrays),
        in_specs=in_vmem(3),
        out_specs=tuple(in_vmem(3)),
    )(*arrays)


def on_device(volume, kernel, upstream):
    weights = kernel.transpose(1, 2, 3, 0, 4).reshape(216, 128)
    pooled, input_grad, total = hand_over(*block(volume, weights, upstream))
    kernel_grad = total.reshape(3, 3, 3, 8, 128).transpose(3, 0, 1, 2, 4)
    return pooled, input_grad, kernel_grad


def solution(mesh):
    return jax.shard_map(
        on_device,
        mesh=mesh,
        in_specs=(
            P("chan", "space", None, None),
            P("chan", None, None, None, None),
            P("chan", "space", None, None),
        ),
        out_specs=(
            P("chan", "space", None, None),
            P("chan", "space", None, None),
            P("chan", None, None, None, None),
        ),
        check_vma=False,
    )
```

```python
import jax
import jax.numpy as jnp
from jax import lax
from jax.experimental import pallas as pl
from jax.experimental.pallas import tpu as pltpu
from jax.sharding import PartitionSpec as P

slope_neg = 0.3
MESH = pl.DeviceIdType.MESH
bf16, f32, i32 = jnp.bfloat16, jnp.float32, jnp.int32


def iota(shape, dim):
    return lax.broadcasted_iota(i32, shape, dim)


def one_hot(condition):
    return jnp.where(condition, 1.0, 0.0).astype(bf16)


def row_picker():
    out, inn = iota((160, 128), 0), iota((160, 128), 1)
    same = (out & 7) == (inn >> 4)
    return one_hot(same & ((inn & 15) == 4 * ((out >> 3) & 3) + (out >> 5) - 1))


def column_picker():
    inn, out = iota((256, 384), 0), iota((256, 384), 1)
    same = (inn >> 7) == ((out >> 6) & 1)
    return one_hot(same & ((inn & 127) == 2 * (out & 63) + (out >> 7) - 1))


def pool_picker():
    coarse, fine = iota((128, 1024), 0), iota((128, 1024), 1)
    return one_hot(
        ((coarse >> 5) == ((fine >> 7) & 3)) & ((coarse & 31) == ((fine >> 1) & 31))
    )


def channel_first():
    out, inn = iota((128, 128), 0), iota((128, 128), 1)
    row = 4 * ((inn >> 3) & 3) + (inn >> 5)
    return one_hot(((out >> 4) == (inn & 7)) & ((out & 15) == row))


def side_by_side(blocks):
    return jnp.concatenate(blocks, axis=1)


def block_kernel(
    n_space,
    vol_in,
    weights_in,
    up_in,
    pooled,
    grad_out,
    total_out,
    vol,
    weights,
    up,
    load,
    rim,
    spread,
    stage,
    taps,
    part,
    from_z,
    z_sum,
    from_y,
    panel,
    rim_panel,
    folds,
    terms,
    got,
    layer_sums,
    mine,
    s_rim,
    r_rim,
    s_z,
    r_z,
    s_y,
    r_y,
    s_gy,
    r_gy,
    s_gz,
    r_gz,
    s_rs,
    r_rs,
    s_up,
    r_up,
    s_ag,
    r_ag,
):
    space, chan = lax.axis_index("space"), lax.axis_index("chan")
    half = lax.div(chan, 8)
    place = lax.rem(chan, 8)
    partner = lax.rem(chan + 8, 16)

    def along(k):
        return half * 8 + lax.rem(place + k, 8)

    def opposite(k):
        return (1 - half) * 8 + lax.rem(place + k, 8)

    def before(k):
        return half * 8 + lax.rem(place + 8 - k, 8)

    def ahead(k):
        return lax.rem(space + k, n_space)

    sent = []

    def send(src, dst, send_sem, recv_sem, **device):
        copy = pltpu.make_async_remote_copy(
            src_ref=src,
            dst_ref=dst,
            send_sem=send_sem,
            recv_sem=recv_sem,
            device_id=device,
            device_id_type=MESH,
        )
        copy.start()
        sent.append(copy)
        return copy

    loads = [
        pltpu.make_async_copy(source, target, load.at[i])
        for i, (source, target) in enumerate(((vol_in, vol), (weights_in, weights), (up_in, up)))
    ]
    for copy in loads:
        copy.start()
    barrier = pltpu.get_barrier_semaphore()
    for k in range(1, 8):
        pl.semaphore_signal(barrier, inc=1, device_id={"chan": along(k)}, device_id_type=MESH)
    for k in (0, 3, 4, 5):
        pl.semaphore_signal(barrier, inc=1, device_id={"chan": opposite(k)}, device_id_type=MESH)
    layers = n_space // 8
    layer = lax.div(space, 8)
    slot = lax.rem(space, 8)

    def beside(m):
        return lax.rem(slot + m, 8)

    for m in range(1, 8):
        peer = layer * 8 + beside(m)
        pl.semaphore_signal(barrier, inc=1, device_id={"space": peer}, device_id_type=MESH)
    for k in [8 * k for k in range(1, layers)] + [1, n_space - 1]:
        pl.semaphore_signal(barrier, inc=1, device_id={"space": ahead(k)}, device_id_type=MESH)

    pick_rows = row_picker()
    pick_cols = column_picker()

    def rows_of(plane):
        return jnp.dot(pick_rows, plane.reshape(128, 128), preferred_element_type=f32)

    for copy in loads:
        copy.wait()
    planes = [None] + [rows_of(vol[:, p]).astype(bf16) for p in range(4)]
    w = weights[...]

    def fill(used, first):
        count = len(used)
        for b in range(3):
            pairs = jnp.concatenate(
                [
                    side_by_side([u[32 * b : 32 * b + 32], u[32 * b + 64 : 32 * b + 96]])
                    for u in used
                ],
                axis=0,
            )
            picked = jnp.dot(pairs, pick_cols, preferred_element_type=f32)
            for e in range(3):
                stage[first : first + count, b * 3 + e] = picked[
                    :, e * 128 : e * 128 + 128
                ].reshape(count, 4, 8, 128)

    def columns_of(count):
        return side_by_side(
            [stage[0:count, :, q].reshape(72 * count, 128) for q in range(4)]
        ).astype(bf16)

    def multiply(rows, columns):
        return lax.dot_general(
            rows, columns, (((0,), (0,)), ((), ())), preferred_element_type=f32
        ).reshape(16, 8, 512)

    far_first = (4, 3, 5, 2, 6, 1, 7)
    z_copies = {}

    def send_half(h):
        for k in far_first + (0,):
            z_copies[h, k] = send(
                part.at[h, opposite(k)], from_z.at[h, k], s_z.at[h, k], r_z.at[h, k], chan=partner
            )

    fill(planes[2:5], 0)
    columns = columns_of(3)
    taps[1] = columns
    part[1] = multiply(w, columns)
    stage[0:1] = jnp.zeros((1, 9, 4, 8, 128), f32)
    fill(planes[1:3], 1)
    part[0] = multiply(w, columns_of(3))
    w_rim = w[0:72]
    coarse = up[...].astype(f32).reshape(8, 4, 32)
    flat = side_by_side([coarse[:, q] for q in range(4)]).astype(bf16)
    spread[...] = jnp.dot(flat, pool_picker(), preferred_element_type=f32) * 0.125
    pl.semaphore_wait(barrier, 7 + 4 + 7 + layers - 1 + 2)
    rim_copy = send(vol.at[:, 3], rim, s_rim.at[0], r_rim.at[0], space=ahead(1))
    send_half(1)
    rim_copy.wait_recv()
    fill([jnp.where(space > 0, rows_of(rim[...]), 0.0).astype(bf16)], 0)
    part[0] = part[0] + multiply(w_rim, columns_of(1))
    send_half(0)
    taps[0] = columns_of(3)

    y_copies = {}
    own = {}
    for h in (1, 0):
        for k in far_first + (0,):
            z_copies[h, k].wait_recv()
            both = part[h, along(k)] + from_z[h, k]
            if k == 0:
                own[h] = both
            else:
                z_sum[h, k] = both
                y_copies[h, k] = send(
                    z_sum.at[h, k], from_y.at[h, k], s_y.at[h, k], r_y.at[h, k], chan=along(k)
                )
    gy, gz = {}, {}
    for h in (1, 0):
        for k in (1, 7, 2, 6, 3, 5, 4):
            y_copies[h, k].wait_recv()
            own[h] = own[h] + from_y[h, k]
        factor = jnp.where(own[h] > 0, 1.0, slope_neg)
        panel[h, chan] = (spread[:, h * 512 : h * 512 + 512] * factor).astype(bf16)
        block = panel.at[h, chan]
        for k in far_first:
            gy[h, k] = send(block, block, s_gy.at[h, k], r_gy.at[h, k], chan=along(k))
        for k in (4, 3, 5, 0):
            gz[h, k] = send(block, block, s_gz.at[h, k], r_gz.at[h, k], chan=opposite(k))
    for h in (1, 0):
        for k in (1, 7, 2, 6):
            gy[h, k].wait_recv()
            block = panel.at[h, before(k)]
            gz[h, k] = send(block, block, s_gz.at[h, k], r_gz.at[h, k], chan=partner)
    across = (((1,), (1,)), ((), ()))
    total = None
    grads = {}
    for h in (1, 0):
        for k in (3, 5, 4):
            gy[h, k].wait_recv()
        for k in range(8):
            gz[h, k].wait_recv()
        grads[h] = panel[h].reshape(128, 512)
        term = lax.dot_general(taps[h], grads[h], across, preferred_element_type=f32)
        total = term if total is None else total + term
    terms[...] = jnp.concatenate([total, jnp.zeros((40, 128), f32)], axis=0).reshape(8, 32, 128)
    rs = []
    for m in (3, 4, 5, 2, 6, 1, 7):
        peer = layer * 8 + beside(m)
        rs.append(send(terms.at[beside(m)], got.at[m], s_rs.at[m], r_rs.at[m], space=peer))

    first_plane = send(
        panel.at[0], rim_panel, s_rim.at[1], r_rim.at[1], space=ahead(n_space - 1)
    )

    for z in range(2):
        for q in range(4):
            folds[z * 4 + q] = jnp.dot(
                w, grads[z][:, q * 128 : q * 128 + 128], preferred_element_type=f32
            ).reshape(27, 8, 128)
    pre = side_by_side([own[0], own[1]])
    act = jnp.where(pre > 0, pre, slope_neg * pre)
    first = act.astype(bf16)
    rest = act - first.astype(f32)
    second = rest.astype(bf16)
    third = (rest - second.astype(f32)).astype(bf16)
    pick = pool_picker()
    mean = sum(
        lax.dot_general(piece, pick, across, preferred_element_type=f32)
        for piece in (third, second, first)
    )
    mean = jnp.stack([mean[:, q * 32 : q * 32 + 32] for q in range(4)], axis=1)
    pooled[...] = (mean * 0.125).astype(bf16).reshape(8, 1, 4, 32)
    share = terms[slot]
    for copy in rs:
        copy.wait_recv()
    for m in range(1, 8):
        share = share + got[m]
    layer_sums[layer] = share
    ups = []
    for k in range(1, layers):
        block = layer_sums.at[layer]
        ups.append(send(block, block, s_up.at[k], r_up.at[k], space=ahead(8 * k)))
    first_plane.wait_recv()
    last = jnp.where(
        space < n_space - 1,
        jnp.dot(w, rim_panel[...].reshape(128, 512), preferred_element_type=f32),
        0.0,
    )
    for q in range(4):
        folds[8 + q] = last[:, q * 128 : q * 128 + 128].reshape(27, 8, 128)
    tall = []
    for b in range(3):
        for a in range(3):
            start = 4 if a == 0 else 0
            tall.append(
                side_by_side(
                    [
                        folds[start : start + 8, a * 9 + b * 3 + e].reshape(64, 128)
                        for e in range(3)
                    ]
                )
            )
    rows = jnp.concatenate(tall, axis=0)
    high = rows.astype(bf16)
    low = (rows - high.astype(f32)).astype(bf16)
    fold = lax.dot_general(high, pick_cols, across, preferred_element_type=f32)
    fold = fold + lax.dot_general(low, pick_cols, across, preferred_element_type=f32)
    for copy in ups:
        copy.wait_recv()
    share = layer_sums[0]
    for k in range(1, layers):
        share = share + layer_sums[k]
    mine[slot] = share
    ag = []
    for m in (3, 4, 5, 2, 6, 1, 7):
        block = mine.at[slot]
        ag.append(send(block, block, s_ag.at[m], r_ag.at[m], space=layer * 8 + beside(m)))
    fold = fold.reshape(3, 3, 2, 4, 8, 256)
    order = channel_first()
    depth_terms = (((1, 0),), ((2, 0), (0, 0)), ((1, 1),), ((2, 1), (0, 1)))
    for i in range(4):
        by_b = []
        for b in range(3):
            acc = None
            for a, zi in depth_terms[i]:
                acc = fold[b, a, zi] if acc is None else acc + fold[b, a, zi]
            by_b.append(acc)
        back, here, on = by_b
        shifted = jnp.concatenate([back[1:, :, :128], jnp.zeros((1, 8, 128), f32)], axis=0)
        plane = jnp.concatenate(
            [
                here[:, :, :128],
                on[:, :, :128] + back[:, :, 128:],
                here[:, :, 128:],
                on[:, :, 128:] + shifted,
            ],
            axis=0,
        ).reshape(128, 128)
        moved = jnp.dot(order, plane.astype(bf16), preferred_element_type=f32)
        grad_out[:, i] = moved.astype(bf16).reshape(8, 16, 128)

    for copy in ag:
        copy.wait_recv()
    for m in range(7):
        total_out[4 * m : min(4 * m + 4, 27)] = mine[m].reshape(4, 8, 128)[: min(4, 27 - 4 * m)]
    for copy in sent:
        copy.wait_send()


def in_vmem(count):
    return [pl.BlockSpec(memory_space=pltpu.VMEM)] * count


def shaped(*shape, dtype=f32):
    return jax.ShapeDtypeStruct(shape, dtype)


def block(vol, weights, up):
    n = lax.axis_size("space")
    dma = pltpu.SemaphoreType.DMA
    return pl.pallas_call(
        lambda *refs: block_kernel(n, *refs),
        name="block",
        out_shape=(
            shaped(8, 1, 4, 32, dtype=bf16),
            shaped(8, 4, 16, 128, dtype=bf16),
            shaped(27, 8, 128),
        ),
        in_specs=[pl.BlockSpec(memory_space=pltpu.HBM)] * 3,
        out_specs=tuple(in_vmem(3)),
        scratch_shapes=[
            pltpu.VMEM((8, 4, 16, 128), bf16),
            pltpu.VMEM((216, 128), bf16),
            pltpu.VMEM((8, 1, 4, 32), bf16),
            dma((3,)),
            pltpu.VMEM((8, 16, 128), bf16),
            pltpu.VMEM((8, 1024), f32),
            pltpu.VMEM((3, 9, 4, 8, 128), f32),
            pltpu.VMEM((2, 216, 512), bf16),
            pltpu.VMEM((2, 16, 8, 512), f32),
            pltpu.VMEM((2, 8, 8, 512), f32),
            pltpu.VMEM((2, 8, 8, 512), f32),
            pltpu.VMEM((2, 8, 8, 512), f32),
            pltpu.VMEM((2, 16, 8, 512), bf16),
            pltpu.VMEM((16, 8, 512), bf16),
            pltpu.VMEM((12, 27, 8, 128), f32),
            pltpu.VMEM((8, 32, 128), f32),
            pltpu.VMEM((8, 32, 128), f32),
            pltpu.VMEM((n // 8, 32, 128), f32),
            pltpu.VMEM((8, 32, 128), f32),
        ]
        + [dma((2,))] * 2
        + [dma((2, 8))] * 8
        + [dma((8,))] * 2
        + [dma((n // 8,))] * 2
        + [dma((8,))] * 2,
        compiler_params=pltpu.CompilerParams(
            collective_id=0, has_side_effects=True, vmem_limit_bytes=24 * 1024 * 1024
        ),
    )(vol, weights, up)


def hand_over(*arrays):
    def kernel(*refs):
        for source, target in zip(refs[:3], refs[3:]):
            target[...] = source[...]

    return pl.pallas_call(
        kernel,
        name="hand_over",
        out_shape=tuple(jax.ShapeDtypeStruct(x.shape, x.dtype) for x in arrays),
        in_specs=in_vmem(3),
        out_specs=tuple(in_vmem(3)),
        compiler_params=pltpu.CompilerParams(vmem_limit_bytes=8 * 1024 * 1024),
    )(*arrays)


def on_device(volume, kernel, upstream):
    weights = kernel.transpose(1, 2, 3, 0, 4).reshape(216, 128)
    held = [
        pltpu.with_memory_space_constraint(x, pltpu.HBM) for x in (volume, weights, upstream)
    ]
    pooled, input_grad, total = hand_over(*block(*held))
    kernel_grad = total.reshape(3, 3, 3, 8, 128).transpose(3, 0, 1, 2, 4)
    return pooled, input_grad, kernel_grad


def solution(mesh):
    return jax.shard_map(
        on_device,
        mesh=mesh,
        in_specs=(
            P("chan", "space", None, None),
            P("chan", None, None, None, None),
            P("chan", "space", None, None),
        ),
        out_specs=(
            P("chan", "space", None, None),
            P("chan", "space", None, None),
            P("chan", None, None, None, None),
        ),
        check_vma=False,
    )
```

```python
import jax
import jax.numpy as jnp
from jax import lax
from jax.experimental import pallas as pl
from jax.experimental.pallas import tpu as pltpu
from jax.sharding import PartitionSpec as P

slope_neg = 0.3
MESH = pl.DeviceIdType.MESH
bf16, f32, i32 = jnp.bfloat16, jnp.float32, jnp.int32


def iota(shape, dim):
    return lax.broadcasted_iota(i32, shape, dim)


def one_hot(condition):
    return jnp.where(condition, 1.0, 0.0).astype(bf16)


def row_picker():
    out, inn = iota((160, 128), 0), iota((160, 128), 1)
    same = (out & 7) == (inn >> 4)
    return one_hot(same & ((inn & 15) == 4 * ((out >> 3) & 3) + (out >> 5) - 1))


def column_picker():
    inn, out = iota((256, 384), 0), iota((256, 384), 1)
    same = (inn >> 7) == ((out >> 6) & 1)
    return one_hot(same & ((inn & 127) == 2 * (out & 63) + (out >> 7) - 1))


def pool_picker():
    coarse, fine = iota((128, 1024), 0), iota((128, 1024), 1)
    return one_hot(
        ((coarse >> 5) == ((fine >> 7) & 3)) & ((coarse & 31) == ((fine >> 1) & 31))
    )


def channel_first():
    out, inn = iota((128, 128), 0), iota((128, 128), 1)
    row = 4 * ((inn >> 3) & 3) + (inn >> 5)
    return one_hot(((out >> 4) == (inn & 7)) & ((out & 15) == row))


def side_by_side(blocks):
    return jnp.concatenate(blocks, axis=1)


def block_kernel(
    n_space,
    vol_in,
    weights_in,
    up_in,
    pooled,
    grad_out,
    total_out,
    vol,
    weights,
    up,
    load,
    rim,
    spread,
    stage,
    taps,
    part,
    from_z,
    z_sum,
    from_y,
    panel,
    rim_panel,
    folds,
    terms,
    got,
    layer_sums,
    mine,
    s_rim,
    r_rim,
    s_z,
    r_z,
    s_y,
    r_y,
    s_gy,
    r_gy,
    s_gz,
    r_gz,
    s_rs,
    r_rs,
    s_up,
    r_up,
    s_ag,
    r_ag,
):
    space, chan = lax.axis_index("space"), lax.axis_index("chan")
    half = lax.div(chan, 8)
    place = lax.rem(chan, 8)
    partner = lax.rem(chan + 8, 16)

    def along(k):
        return half * 8 + lax.rem(place + k, 8)

    def opposite(k):
        return (1 - half) * 8 + lax.rem(place + k, 8)

    def before(k):
        return half * 8 + lax.rem(place + 8 - k, 8)

    def ahead(k):
        return lax.rem(space + k, n_space)

    sent = []

    def send(src, dst, send_sem, recv_sem, **device):
        copy = pltpu.make_async_remote_copy(
            src_ref=src,
            dst_ref=dst,
            send_sem=send_sem,
            recv_sem=recv_sem,
            device_id=device,
            device_id_type=MESH,
        )
        copy.start()
        sent.append(copy)
        return copy

    loads = [
        pltpu.make_async_copy(source, target, load.at[i])
        for i, (source, target) in enumerate(((vol_in, vol), (weights_in, weights), (up_in, up)))
    ]
    for copy in loads:
        copy.start()
    barrier = pltpu.get_barrier_semaphore()
    for k in range(1, 8):
        pl.semaphore_signal(barrier, inc=1, device_id={"chan": along(k)}, device_id_type=MESH)
    for k in (0, 3, 4, 5):
        pl.semaphore_signal(barrier, inc=1, device_id={"chan": opposite(k)}, device_id_type=MESH)
    layers = n_space // 8
    layer = lax.div(space, 8)
    slot = lax.rem(space, 8)

    def beside(m):
        return lax.rem(slot + m, 8)

    for m in range(1, 8):
        peer = layer * 8 + beside(m)
        pl.semaphore_signal(barrier, inc=1, device_id={"space": peer}, device_id_type=MESH)
    for k in [8 * k for k in range(1, layers)] + [1, n_space - 1]:
        pl.semaphore_signal(barrier, inc=1, device_id={"space": ahead(k)}, device_id_type=MESH)

    pick_rows = row_picker()
    pick_cols = column_picker()

    def rows_of(plane):
        return jnp.dot(pick_rows, plane.reshape(128, 128), preferred_element_type=f32)

    for copy in loads:
        copy.wait()
    planes = [None] + [rows_of(vol[:, p]).astype(bf16) for p in range(4)]
    w = weights[...]

    def fill(used, first):
        count = len(used)
        for b in range(3):
            pairs = jnp.concatenate(
                [
                    side_by_side([u[32 * b : 32 * b + 32], u[32 * b + 64 : 32 * b + 96]])
                    for u in used
                ],
                axis=0,
            )
            picked = jnp.dot(pairs, pick_cols, preferred_element_type=f32)
            for e in range(3):
                stage[first : first + count, b * 3 + e] = picked[
                    :, e * 128 : e * 128 + 128
                ].reshape(count, 4, 8, 128)

    def columns_of(count):
        return side_by_side(
            [stage[0:count, :, q].reshape(72 * count, 128) for q in range(4)]
        ).astype(bf16)

    def multiply(rows, columns):
        return lax.dot_general(
            rows, columns, (((0,), (0,)), ((), ())), preferred_element_type=f32
        ).reshape(16, 8, 512)

    far_first = (4, 3, 5, 2, 6, 1, 7)
    z_copies = {}

    def send_half(h):
        for k in far_first + (0,):
            z_copies[h, k] = send(
                part.at[h, opposite(k)], from_z.at[h, k], s_z.at[h, k], r_z.at[h, k], chan=partner
            )

    fill(planes[2:5], 0)
    columns = columns_of(3)
    taps[1] = columns
    part[1] = multiply(w, columns)
    pl.semaphore_wait(barrier, 7 + 4 + 7 + layers - 1 + 2)
    rim_copy = send(vol.at[:, 3], rim, s_rim.at[0], r_rim.at[0], space=ahead(1))
    send_half(1)
    stage[0:1] = jnp.zeros((1, 9, 4, 8, 128), f32)
    fill(planes[1:3], 1)
    part[0] = multiply(w, columns_of(3))
    w_rim = w[0:72]
    coarse = up[...].astype(f32).reshape(8, 4, 32)
    flat = side_by_side([coarse[:, q] for q in range(4)]).astype(bf16)
    spread[...] = jnp.dot(flat, pool_picker(), preferred_element_type=f32) * 0.125
    rim_copy.wait_recv()
    fill([jnp.where(space > 0, rows_of(rim[...]), 0.0).astype(bf16)], 0)
    part[0] = part[0] + multiply(w_rim, columns_of(1))
    send_half(0)
    taps[0] = columns_of(3)

    y_copies = {}
    own = {}
    for h in (1, 0):
        for k in far_first + (0,):
            z_copies[h, k].wait_recv()
            both = part[h, along(k)] + from_z[h, k]
            if k == 0:
                own[h] = both
            else:
                z_sum[h, k] = both
                y_copies[h, k] = send(
                    z_sum.at[h, k], from_y.at[h, k], s_y.at[h, k], r_y.at[h, k], chan=along(k)
                )
    gy, gz = {}, {}
    for h in (1, 0):
        for k in (1, 7, 2, 6, 3, 5, 4):
            y_copies[h, k].wait_recv()
            own[h] = own[h] + from_y[h, k]
        factor = jnp.where(own[h] > 0, 1.0, slope_neg)
        panel[h, chan] = (spread[:, h * 512 : h * 512 + 512] * factor).astype(bf16)
        block = panel.at[h, chan]
        for k in (4, 3, 5):
            gz[h, k] = send(block, block, s_gz.at[h, k], r_gz.at[h, k], chan=opposite(k))
        for k in (2, 6, 4, 3, 5, 1, 7):
            gy[h, k] = send(block, block, s_gy.at[h, k], r_gy.at[h, k], chan=along(k))
        gz[h, 0] = send(block, block, s_gz.at[h, 0], r_gz.at[h, 0], chan=partner)
    for h in (1, 0):
        for k in (1, 7, 2, 6):
            gy[h, k].wait_recv()
            block = panel.at[h, before(k)]
            gz[h, k] = send(block, block, s_gz.at[h, k], r_gz.at[h, k], chan=partner)
    across = (((1,), (1,)), ((), ()))
    total = None
    grads = {}
    for h in (1, 0):
        for k in (3, 5, 4):
            gy[h, k].wait_recv()
        for k in range(8):
            gz[h, k].wait_recv()
        grads[h] = panel[h].reshape(128, 512)
        term = lax.dot_general(taps[h], grads[h], across, preferred_element_type=f32)
        total = term if total is None else total + term
    terms[...] = jnp.concatenate([total, jnp.zeros((40, 128), f32)], axis=0).reshape(8, 32, 128)
    rs = []
    for m in (3, 4, 5, 2, 6, 1, 7):
        peer = layer * 8 + beside(m)
        rs.append(send(terms.at[beside(m)], got.at[m], s_rs.at[m], r_rs.at[m], space=peer))

    first_plane = send(
        panel.at[0], rim_panel, s_rim.at[1], r_rim.at[1], space=ahead(n_space - 1)
    )

    for z in range(2):
        for q in range(4):
            folds[z * 4 + q] = jnp.dot(
                w, grads[z][:, q * 128 : q * 128 + 128], preferred_element_type=f32
            ).reshape(27, 8, 128)
    pre = side_by_side([own[0], own[1]])
    act = jnp.where(pre > 0, pre, slope_neg * pre)
    first = act.astype(bf16)
    rest = act - first.astype(f32)
    second = rest.astype(bf16)
    third = (rest - second.astype(f32)).astype(bf16)
    pick = pool_picker()
    mean = sum(
        lax.dot_general(piece, pick, across, preferred_element_type=f32)
        for piece in (third, second, first)
    )
    mean = jnp.stack([mean[:, q * 32 : q * 32 + 32] for q in range(4)], axis=1)
    pooled[...] = (mean * 0.125).astype(bf16).reshape(8, 1, 4, 32)
    share = terms[slot]
    for copy in rs:
        copy.wait_recv()
    for m in range(1, 8):
        share = share + got[m]
    layer_sums[layer] = share
    ups = []
    for k in range(1, layers):
        block = layer_sums.at[layer]
        ups.append(send(block, block, s_up.at[k], r_up.at[k], space=ahead(8 * k)))
    first_plane.wait_recv()
    last = jnp.where(
        space < n_space - 1,
        jnp.dot(w, rim_panel[...].reshape(128, 512), preferred_element_type=f32),
        0.0,
    )
    for q in range(4):
        folds[8 + q] = last[:, q * 128 : q * 128 + 128].reshape(27, 8, 128)
    tall = []
    for b in range(3):
        for a in range(3):
            start = 4 if a == 0 else 0
            tall.append(
                side_by_side(
                    [
                        folds[start : start + 8, a * 9 + b * 3 + e].reshape(64, 128)
                        for e in range(3)
                    ]
                )
            )
    rows = jnp.concatenate(tall, axis=0)
    high = rows.astype(bf16)
    low = (rows - high.astype(f32)).astype(bf16)
    fold = lax.dot_general(high, pick_cols, across, preferred_element_type=f32)
    fold = fold + lax.dot_general(low, pick_cols, across, preferred_element_type=f32)
    for copy in ups:
        copy.wait_recv()
    share = layer_sums[0]
    for k in range(1, layers):
        share = share + layer_sums[k]
    mine[slot] = share
    ag = []
    for m in (3, 4, 5, 2, 6, 1, 7):
        block = mine.at[slot]
        ag.append(send(block, block, s_ag.at[m], r_ag.at[m], space=layer * 8 + beside(m)))
    fold = fold.reshape(3, 3, 2, 4, 8, 256)
    order = channel_first()
    depth_terms = (((1, 0),), ((2, 0), (0, 0)), ((1, 1),), ((2, 1), (0, 1)))
    for i in range(4):
        by_b = []
        for b in range(3):
            acc = None
            for a, zi in depth_terms[i]:
                acc = fold[b, a, zi] if acc is None else acc + fold[b, a, zi]
            by_b.append(acc)
        back, here, on = by_b
        shifted = jnp.concatenate([back[1:, :, :128], jnp.zeros((1, 8, 128), f32)], axis=0)
        plane = jnp.concatenate(
            [
                here[:, :, :128],
                on[:, :, :128] + back[:, :, 128:],
                here[:, :, 128:],
                on[:, :, 128:] + shifted,
            ],
            axis=0,
        ).reshape(128, 128)
        moved = jnp.dot(order, plane.astype(bf16), preferred_element_type=f32)
        grad_out[:, i] = moved.astype(bf16).reshape(8, 16, 128)

    for copy in ag:
        copy.wait_recv()
    for m in range(7):
        total_out[4 * m : min(4 * m + 4, 27)] = mine[m].reshape(4, 8, 128)[: min(4, 27 - 4 * m)]
    for copy in sent:
        copy.wait_send()


def in_vmem(count):
    return [pl.BlockSpec(memory_space=pltpu.VMEM)] * count


def shaped(*shape, dtype=f32):
    return jax.ShapeDtypeStruct(shape, dtype)


def block(vol, weights, up):
    n = lax.axis_size("space")
    dma = pltpu.SemaphoreType.DMA
    return pl.pallas_call(
        lambda *refs: block_kernel(n, *refs),
        name="block",
        out_shape=(
            shaped(8, 1, 4, 32, dtype=bf16),
            shaped(8, 4, 16, 128, dtype=bf16),
            shaped(27, 8, 128),
        ),
        in_specs=[pl.BlockSpec(memory_space=pltpu.HBM)] * 3,
        out_specs=tuple(in_vmem(3)),
        scratch_shapes=[
            pltpu.VMEM((8, 4, 16, 128), bf16),
            pltpu.VMEM((216, 128), bf16),
            pltpu.VMEM((8, 1, 4, 32), bf16),
            dma((3,)),
            pltpu.VMEM((8, 16, 128), bf16),
            pltpu.VMEM((8, 1024), f32),
            pltpu.VMEM((3, 9, 4, 8, 128), f32),
            pltpu.VMEM((2, 216, 512), bf16),
            pltpu.VMEM((2, 16, 8, 512), f32),
            pltpu.VMEM((2, 8, 8, 512), f32),
            pltpu.VMEM((2, 8, 8, 512), f32),
            pltpu.VMEM((2, 8, 8, 512), f32),
            pltpu.VMEM((2, 16, 8, 512), bf16),
            pltpu.VMEM((16, 8, 512), bf16),
            pltpu.VMEM((12, 27, 8, 128), f32),
            pltpu.VMEM((8, 32, 128), f32),
            pltpu.VMEM((8, 32, 128), f32),
            pltpu.VMEM((n // 8, 32, 128), f32),
            pltpu.VMEM((8, 32, 128), f32),
        ]
        + [dma((2,))] * 2
        + [dma((2, 8))] * 8
        + [dma((8,))] * 2
        + [dma((n // 8,))] * 2
        + [dma((8,))] * 2,
        compiler_params=pltpu.CompilerParams(
            collective_id=0, has_side_effects=True, vmem_limit_bytes=24 * 1024 * 1024
        ),
    )(vol, weights, up)


def hand_over(*arrays):
    def kernel(*refs):
        for source, target in zip(refs[:3], refs[3:]):
            target[...] = source[...]

    return pl.pallas_call(
        kernel,
        name="hand_over",
        out_shape=tuple(jax.ShapeDtypeStruct(x.shape, x.dtype) for x in arrays),
        in_specs=in_vmem(3),
        out_specs=tuple(in_vmem(3)),
        compiler_params=pltpu.CompilerParams(vmem_limit_bytes=8 * 1024 * 1024),
    )(*arrays)


def on_device(volume, kernel, upstream):
    weights = kernel.transpose(1, 2, 3, 0, 4).reshape(216, 128)
    held = [
        pltpu.with_memory_space_constraint(x, pltpu.HBM) for x in (volume, weights, upstream)
    ]
    pooled, input_grad, total = hand_over(*block(*held))
    kernel_grad = total.reshape(3, 3, 3, 8, 128).transpose(3, 0, 1, 2, 4)
    return pooled, input_grad, kernel_grad


def solution(mesh):
    return jax.shard_map(
        on_device,
        mesh=mesh,
        in_specs=(
            P("chan", "space", None, None),
            P("chan", None, None, None, None),
            P("chan", "space", None, None),
        ),
        out_specs=(
            P("chan", "space", None, None),
            P("chan", "space", None, None),
            P("chan", None, None, None, None),
        ),
        check_vma=False,
    )
```

```python
import jax
import jax.numpy as jnp
from jax import lax
from jax.experimental import pallas as pl
from jax.experimental.pallas import tpu as pltpu
from jax.sharding import PartitionSpec as P

slope_neg = 0.3
MESH = pl.DeviceIdType.MESH
bf16, f32, i32 = jnp.bfloat16, jnp.float32, jnp.int32


def iota(shape, dim):
    return lax.broadcasted_iota(i32, shape, dim)


def one_hot(condition):
    return jnp.where(condition, 1.0, 0.0).astype(bf16)


def row_picker():
    out, inn = iota((160, 128), 0), iota((160, 128), 1)
    same = (out & 7) == (inn >> 4)
    return one_hot(same & ((inn & 15) == 4 * ((out >> 3) & 3) + (out >> 5) - 1))


def column_picker():
    inn, out = iota((256, 384), 0), iota((256, 384), 1)
    same = (inn >> 7) == ((out >> 6) & 1)
    return one_hot(same & ((inn & 127) == 2 * (out & 63) + (out >> 7) - 1))


def pool_picker():
    coarse, fine = iota((128, 1024), 0), iota((128, 1024), 1)
    return one_hot(
        ((coarse >> 5) == ((fine >> 7) & 3)) & ((coarse & 31) == ((fine >> 1) & 31))
    )


def channel_first():
    out, inn = iota((128, 128), 0), iota((128, 128), 1)
    row = 4 * ((inn >> 3) & 3) + (inn >> 5)
    return one_hot(((out >> 4) == (inn & 7)) & ((out & 15) == row))


def side_by_side(blocks):
    return jnp.concatenate(blocks, axis=1)


def block_kernel(
    n_space,
    vol_in,
    weights_in,
    up_in,
    pooled,
    grad_out,
    total_out,
    vol,
    weights,
    up,
    load,
    rim,
    spread,
    stage,
    taps,
    part,
    from_z,
    z_sum,
    from_y,
    panel,
    rim_panel,
    folds,
    terms,
    got,
    layer_sums,
    mine,
    s_rim,
    r_rim,
    s_z,
    r_z,
    s_y,
    r_y,
    s_gy,
    r_gy,
    s_gz,
    r_gz,
    s_rs,
    r_rs,
    s_up,
    r_up,
    s_ag,
    r_ag,
):
    space, chan = lax.axis_index("space"), lax.axis_index("chan")
    half = lax.div(chan, 8)
    place = lax.rem(chan, 8)
    partner = lax.rem(chan + 8, 16)

    def along(k):
        return half * 8 + lax.rem(place + k, 8)

    def opposite(k):
        return (1 - half) * 8 + lax.rem(place + k, 8)

    def before(k):
        return half * 8 + lax.rem(place + 8 - k, 8)

    def ahead(k):
        return lax.rem(space + k, n_space)

    sent = []

    def send(src, dst, send_sem, recv_sem, **device):
        copy = pltpu.make_async_remote_copy(
            src_ref=src,
            dst_ref=dst,
            send_sem=send_sem,
            recv_sem=recv_sem,
            device_id=device,
            device_id_type=MESH,
        )
        copy.start()
        sent.append(copy)
        return copy

    loads = [
        pltpu.make_async_copy(source, target, load.at[i])
        for i, (source, target) in enumerate(((vol_in, vol), (weights_in, weights), (up_in, up)))
    ]
    for copy in loads:
        copy.start()
    barrier = pltpu.get_barrier_semaphore()
    for k in range(1, 8):
        pl.semaphore_signal(barrier, inc=1, device_id={"chan": along(k)}, device_id_type=MESH)
    for k in (0, 3, 4, 5):
        pl.semaphore_signal(barrier, inc=1, device_id={"chan": opposite(k)}, device_id_type=MESH)
    layers = n_space // 8
    layer = lax.div(space, 8)
    slot = lax.rem(space, 8)

    def beside(m):
        return lax.rem(slot + m, 8)

    for m in range(1, 8):
        peer = layer * 8 + beside(m)
        pl.semaphore_signal(barrier, inc=1, device_id={"space": peer}, device_id_type=MESH)
    for k in [8 * k for k in range(1, layers)] + [1, n_space - 1]:
        pl.semaphore_signal(barrier, inc=1, device_id={"space": ahead(k)}, device_id_type=MESH)

    pick_rows = row_picker()
    pick_cols = column_picker()

    def rows_of(plane):
        return jnp.dot(pick_rows, plane.reshape(128, 128), preferred_element_type=f32)

    for copy in loads:
        copy.wait()
    planes = [None] + [rows_of(vol[:, p]).astype(bf16) for p in range(4)]
    w = weights[...]

    def fill(used, first):
        count = len(used)
        for b in range(3):
            pairs = jnp.concatenate(
                [
                    side_by_side([u[32 * b : 32 * b + 32], u[32 * b + 64 : 32 * b + 96]])
                    for u in used
                ],
                axis=0,
            )
            picked = jnp.dot(pairs, pick_cols, preferred_element_type=f32)
            for e in range(3):
                stage[first : first + count, b * 3 + e] = picked[
                    :, e * 128 : e * 128 + 128
                ].reshape(count, 4, 8, 128)

    def columns_of(count):
        return side_by_side(
            [stage[0:count, :, q].reshape(72 * count, 128) for q in range(4)]
        ).astype(bf16)

    def multiply(rows, columns):
        return lax.dot_general(
            rows, columns, (((0,), (0,)), ((), ())), preferred_element_type=f32
        ).reshape(16, 8, 512)

    far_first = (4, 3, 5, 2, 6, 1, 7)
    z_copies = {}

    def send_half(h):
        for k in far_first + (0,):
            z_copies[h, k] = send(
                part.at[h, opposite(k)], from_z.at[h, k], s_z.at[h, k], r_z.at[h, k], chan=partner
            )

    fill(planes[2:5], 0)
    columns = columns_of(3)
    taps[1] = columns
    part[1] = multiply(w, columns)
    pl.semaphore_wait(barrier, 7 + 4 + 7 + layers - 1 + 2)
    rim_copy = send(vol.at[:, 3], rim, s_rim.at[0], r_rim.at[0], space=ahead(1))
    send_half(1)
    stage[0:1] = jnp.zeros((1, 9, 4, 8, 128), f32)
    fill(planes[1:3], 1)
    part[0] = multiply(w, columns_of(3))
    w_rim = w[0:72]
    coarse = up[...].astype(f32).reshape(8, 4, 32)
    flat = side_by_side([coarse[:, q] for q in range(4)]).astype(bf16)
    spread[...] = jnp.dot(flat, pool_picker(), preferred_element_type=f32) * 0.125
    rim_copy.wait_recv()
    fill([jnp.where(space > 0, rows_of(rim[...]), 0.0).astype(bf16)], 0)
    part[0] = part[0] + multiply(w_rim, columns_of(1))
    send_half(0)
    taps[0] = columns_of(3)

    y_copies = {}
    own = {}
    for h in (1, 0):
        for k in far_first + (0,):
            z_copies[h, k].wait_recv()
            both = part[h, along(k)] + from_z[h, k]
            if k == 0:
                own[h] = both
            else:
                z_sum[h, k] = both
                y_copies[h, k] = send(
                    z_sum.at[h, k], from_y.at[h, k], s_y.at[h, k], r_y.at[h, k], chan=along(k)
                )
    gy, gz = {}, {}
    for h in (1, 0):
        for k in (1, 7, 2, 6, 3, 5, 4):
            y_copies[h, k].wait_recv()
            own[h] = own[h] + from_y[h, k]
        factor = jnp.where(own[h] > 0, 1.0, slope_neg)
        panel[h, chan] = (spread[:, h * 512 : h * 512 + 512] * factor).astype(bf16)
        block = panel.at[h, chan]
        for k in (4, 3, 5):
            gz[h, k] = send(block, block, s_gz.at[h, k], r_gz.at[h, k], chan=opposite(k))
        for k in (2, 6, 4, 3, 5, 1, 7):
            gy[h, k] = send(block, block, s_gy.at[h, k], r_gy.at[h, k], chan=along(k))
        gz[h, 0] = send(block, block, s_gz.at[h, 0], r_gz.at[h, 0], chan=partner)
    for h in (1, 0):
        for k in (1, 7, 2, 6):
            gy[h, k].wait_recv()
            block = panel.at[h, before(k)]
            gz[h, k] = send(block, block, s_gz.at[h, k], r_gz.at[h, k], chan=partner)
    across = (((1,), (1,)), ((), ()))
    total = None
    grads = {}
    for h in (1, 0):
        for k in (3, 5, 4):
            gy[h, k].wait_recv()
        for k in range(8):
            gz[h, k].wait_recv()
        grads[h] = panel[h].reshape(128, 512)
        term = lax.dot_general(taps[h], grads[h], across, preferred_element_type=f32)
        total = term if total is None else total + term
    terms[...] = jnp.concatenate([total, jnp.zeros((40, 128), f32)], axis=0).reshape(8, 32, 128)
    rs = []
    for m in (3, 4, 5, 2, 6, 1, 7):
        peer = layer * 8 + beside(m)
        rs.append(send(terms.at[beside(m)], got.at[m], s_rs.at[m], r_rs.at[m], space=peer))

    first_plane = send(
        panel.at[0], rim_panel, s_rim.at[1], r_rim.at[1], space=ahead(n_space - 1)
    )

    for z in range(2):
        for q in range(4):
            folds[z * 4 + q] = jnp.dot(
                w, grads[z][:, q * 128 : q * 128 + 128], preferred_element_type=f32
            ).reshape(27, 8, 128)
    share = terms[slot]
    for copy in rs:
        copy.wait_recv()
    for m in range(1, 8):
        share = share + got[m]
    layer_sums[layer] = share
    ups = []
    for k in range(1, layers):
        block = layer_sums.at[layer]
        ups.append(send(block, block, s_up.at[k], r_up.at[k], space=ahead(8 * k)))
    first_plane.wait_recv()
    last = jnp.where(
        space < n_space - 1,
        jnp.dot(w, rim_panel[...].reshape(128, 512), preferred_element_type=f32),
        0.0,
    )
    for q in range(4):
        folds[8 + q] = last[:, q * 128 : q * 128 + 128].reshape(27, 8, 128)
    tall = []
    for b in range(3):
        for a in range(3):
            start = 4 if a == 0 else 0
            tall.append(
                side_by_side(
                    [
                        folds[start : start + 8, a * 9 + b * 3 + e].reshape(64, 128)
                        for e in range(3)
                    ]
                )
            )
    rows = jnp.concatenate(tall, axis=0)
    high = rows.astype(bf16)
    low = (rows - high.astype(f32)).astype(bf16)
    fold = lax.dot_general(high, pick_cols, across, preferred_element_type=f32)
    fold = fold + lax.dot_general(low, pick_cols, across, preferred_element_type=f32)
    for copy in ups:
        copy.wait_recv()
    share = layer_sums[0]
    for k in range(1, layers):
        share = share + layer_sums[k]
    mine[slot] = share
    ag = []
    for m in (3, 4, 5, 2, 6, 1, 7):
        block = mine.at[slot]
        ag.append(send(block, block, s_ag.at[m], r_ag.at[m], space=layer * 8 + beside(m)))
    pre = side_by_side([own[0], own[1]])
    act = jnp.where(pre > 0, pre, slope_neg * pre)
    first = act.astype(bf16)
    rest = act - first.astype(f32)
    second = rest.astype(bf16)
    third = (rest - second.astype(f32)).astype(bf16)
    pick = pool_picker()
    mean = sum(
        lax.dot_general(piece, pick, across, preferred_element_type=f32)
        for piece in (third, second, first)
    )
    mean = jnp.stack([mean[:, q * 32 : q * 32 + 32] for q in range(4)], axis=1)
    pooled[...] = (mean * 0.125).astype(bf16).reshape(8, 1, 4, 32)
    fold = fold.reshape(3, 3, 2, 4, 8, 256)
    order = channel_first()
    depth_terms = (((1, 0),), ((2, 0), (0, 0)), ((1, 1),), ((2, 1), (0, 1)))
    for i in range(4):
        by_b = []
        for b in range(3):
            acc = None
            for a, zi in depth_terms[i]:
                acc = fold[b, a, zi] if acc is None else acc + fold[b, a, zi]
            by_b.append(acc)
        back, here, on = by_b
        shifted = jnp.concatenate([back[1:, :, :128], jnp.zeros((1, 8, 128), f32)], axis=0)
        plane = jnp.concatenate(
            [
                here[:, :, :128],
                on[:, :, :128] + back[:, :, 128:],
                here[:, :, 128:],
                on[:, :, 128:] + shifted,
            ],
            axis=0,
        ).reshape(128, 128)
        moved = jnp.dot(order, plane.astype(bf16), preferred_element_type=f32)
        grad_out[:, i] = moved.astype(bf16).reshape(8, 16, 128)

    for copy in ag:
        copy.wait_recv()
    for m in range(7):
        total_out[4 * m : min(4 * m + 4, 27)] = mine[m].reshape(4, 8, 128)[: min(4, 27 - 4 * m)]
    for copy in sent:
        copy.wait_send()


def in_vmem(count):
    return [pl.BlockSpec(memory_space=pltpu.VMEM)] * count


def shaped(*shape, dtype=f32):
    return jax.ShapeDtypeStruct(shape, dtype)


def block(vol, weights, up):
    n = lax.axis_size("space")
    dma = pltpu.SemaphoreType.DMA
    return pl.pallas_call(
        lambda *refs: block_kernel(n, *refs),
        name="block",
        out_shape=(
            shaped(8, 1, 4, 32, dtype=bf16),
            shaped(8, 4, 16, 128, dtype=bf16),
            shaped(27, 8, 128),
        ),
        in_specs=[pl.BlockSpec(memory_space=pltpu.HBM)] * 3,
        out_specs=tuple(in_vmem(3)),
        scratch_shapes=[
            pltpu.VMEM((8, 4, 16, 128), bf16),
            pltpu.VMEM((216, 128), bf16),
            pltpu.VMEM((8, 1, 4, 32), bf16),
            dma((3,)),
            pltpu.VMEM((8, 16, 128), bf16),
            pltpu.VMEM((8, 1024), f32),
            pltpu.VMEM((3, 9, 4, 8, 128), f32),
            pltpu.VMEM((2, 216, 512), bf16),
            pltpu.VMEM((2, 16, 8, 512), f32),
            pltpu.VMEM((2, 8, 8, 512), f32),
            pltpu.VMEM((2, 8, 8, 512), f32),
            pltpu.VMEM((2, 8, 8, 512), f32),
            pltpu.VMEM((2, 16, 8, 512), bf16),
            pltpu.VMEM((16, 8, 512), bf16),
            pltpu.VMEM((12, 27, 8, 128), f32),
            pltpu.VMEM((8, 32, 128), f32),
            pltpu.VMEM((8, 32, 128), f32),
            pltpu.VMEM((n // 8, 32, 128), f32),
            pltpu.VMEM((8, 32, 128), f32),
        ]
        + [dma((2,))] * 2
        + [dma((2, 8))] * 8
        + [dma((8,))] * 2
        + [dma((n // 8,))] * 2
        + [dma((8,))] * 2,
        compiler_params=pltpu.CompilerParams(
            collective_id=0, has_side_effects=True, vmem_limit_bytes=24 * 1024 * 1024
        ),
    )(vol, weights, up)


def hand_over(*arrays):
    def kernel(*refs):
        for source, target in zip(refs[:3], refs[3:]):
            target[...] = source[...]

    return pl.pallas_call(
        kernel,
        name="hand_over",
        out_shape=tuple(jax.ShapeDtypeStruct(x.shape, x.dtype) for x in arrays),
        in_specs=in_vmem(3),
        out_specs=tuple(in_vmem(3)),
        compiler_params=pltpu.CompilerParams(vmem_limit_bytes=8 * 1024 * 1024),
    )(*arrays)


def on_device(volume, kernel, upstream):
    weights = kernel.transpose(1, 2, 3, 0, 4).reshape(216, 128)
    held = [
        pltpu.with_memory_space_constraint(x, pltpu.HBM) for x in (volume, weights, upstream)
    ]
    pooled, input_grad, total = hand_over(*block(*held))
    kernel_grad = total.reshape(3, 3, 3, 8, 128).transpose(3, 0, 1, 2, 4)
    return pooled, input_grad, kernel_grad


def solution(mesh):
    return jax.shard_map(
        on_device,
        mesh=mesh,
        in_specs=(
            P("chan", "space", None, None),
            P("chan", None, None, None, None),
            P("chan", "space", None, None),
        ),
        out_specs=(
            P("chan", "space", None, None),
            P("chan", "space", None, None),
            P("chan", None, None, None, None),
        ),
        check_vma=False,
    )
```
